32 devices in a mesh: req: 4 (over y, x), seq: 8 (over z, core).
Axes of the slice: x: 2, y: 2, z: 4, core: 2. Of those that a mesh axis runs over, the one named last changes fastest.
Arguments:
- residual: bfloat16 [64, 2048], P(None, ('req', 'seq')), may hold values from -90 to 90
- query_plain: bfloat16 [64, 16, 128], P('req'), may hold values from -6 to 6
- query_rotary: bfloat16 [64, 16, 64], P('req'), may hold values from -110 to 110
- latent_cache: bfloat16 [64, 3072, 512], P('req', 'seq'), may hold values from -9 to 9
- rotary_cache: bfloat16 [64, 64, 3072], P('req', None, 'seq'), may hold values from -4.5 to 4.5
- lengths: int32 [64], P('req'), may hold values from 2 to 3072, as said below
- absorb_key: bfloat16 [16, 128, 512], replicated, may hold values from -0.5 to 0.5
- absorb_value: bfloat16 [16, 512, 128], replicated, may hold values from -0.25 to 0.25
- output_weight: bfloat16 [2048, 2048], P(None, ('req', 'seq')), may hold values from -0.125 to 0.125
- middle_gain: float32 [2048], replicated, may hold values from 0.5 to 1.5
- routes: int32 [64, 6], replicated, may hold values from 0 to 63, all different within a row
- route_weights: float32 [64, 6], replicated, may hold values from 0.05 to 0.45
- gate_weight: bfloat16 [64, 2048, 1408], P('seq', None, 'req'), may hold values from -0.125 to 0.125
- up_weight: bfloat16 [64, 2048, 1408], P('seq', None, 'req'), may hold values from -0.125 to 0.125
- down_weight: bfloat16 [64, 1408, 2048], P('seq', 'req'), may hold values from -0.15625 to 0.15625
- shared_gate: bfloat16 [2048, 2816], P(None, ('req', 'seq')), may hold values from -0.125 to 0.125
- shared_up: bfloat16 [2048, 2816], P(None, ('req', 'seq')), may hold values from -0.125 to 0.125
- shared_down: bfloat16 [2816, 2048], P(('req', 'seq')), may hold values from -0.109375 to 0.109375
- final_gain: float32 [2048], replicated, may hold values from 0.5 to 1.5
- unembed: bfloat16 [102400, 2048], P(('req', 'seq')), may hold values from -0.65115609 to 0.65115609
Outputs:
- layer_out: bfloat16 [64, 2048], P(None, ('req', 'seq'))
- best_logits: float32 [64, 2], replicated
The draws below stay inside these ranges and needn't reach their ends.
Inputs may be any that keep to these rules, and one draw needn't show every extreme that they name: Request r uses cache positions 0 to lengths[r] - 1, the new token's entry included; in every draw some request's cache is full.
All inputs are finite; a program needn't handle non-finite values.
Results may differ from the reference program's by a relative error of at most 0.0095.
Values may be sent and summed in bfloat16 or wider, within the bound.
A program may use at most 128 MiB of HBM per device.

```python
import math
import jax
import jax.numpy as jnp
from jax import lax

D = 2048
HEADS = 16
NOPE = 128
ROPE = 64
VDIM = 128
LATENT = 512
EXPERTS = 64
FF_E = 1408
TOPK = 6
VOCAB = 102400
CTX_DEV = 384
REQS = 64
MAX_LEN = 3072
SHARED_FF = 2816


def residual_parts(key):
    base_key = jax.random.fold_in(key, 101)
    row_key, column_key, body_key = jax.random.split(base_key, 3)
    column_place = jnp.arange(D, dtype=jnp.float32) / (D - 1)
    row_scale = jnp.exp(jax.random.uniform(row_key, (REQS, 1), jnp.float32, math.log(0.3), math.log(3.0)))
    column_scale = jnp.exp(jax.random.uniform(column_key, (1, D), jnp.float32, math.log(0.3), math.log(3.0)))
    column_scale = column_scale * jnp.exp(0.5 * math.log(3.0) * column_place)[None, :]
    pattern = jax.random.truncated_normal(body_key, -4.0, 4.0, (REQS, D), jnp.float32)
    return (row_scale, column_scale, pattern)


def draw_residual(key, part):
    row_scale, column_scale, pattern = residual_parts(key)
    return (row_scale * column_scale * pattern).astype(jnp.bfloat16)


def draw_unembed(key, part):
    row_scale, column_scale, pattern = residual_parts(key)
    noise_key = jax.random.fold_in(key, 202)
    place_key = jax.random.fold_in(key, 606)
    level_key = jax.random.fold_in(key, 707)
    noise = jax.random.truncated_normal(noise_key, -4.5, 4.5, (VOCAB, D), jnp.float32)
    noise = noise * (3.0 / math.sqrt(D))
    planted_count = 2 * REQS
    first_level = jnp.full((REQS,), 32.0, jnp.float32)
    second_level = jax.random.uniform(level_key, (REQS,), jnp.float32, 3.0, 10.0)
    amplitude = jnp.concatenate([first_level, second_level])
    planted = amplitude[:, None] * jnp.tile(column_scale * pattern, (2, 1)) / D
    planted_rows = jax.random.permutation(place_key, VOCAB)[:planted_count]
    return noise.at[planted_rows].add(planted).astype(jnp.bfloat16)


def draw_latent_cache(key, part):
    base_key = jax.random.fold_in(key, 303)
    body_key, factor_key = jax.random.split(base_key)
    pattern = jax.random.truncated_normal(body_key, -4.5, 4.5, (REQS, MAX_LEN, LATENT), jnp.float32)
    factor = jnp.exp(jax.random.uniform(factor_key, (REQS, MAX_LEN, 1), jnp.float32, math.log(0.5), math.log(2.0)))
    return (pattern * factor).astype(jnp.bfloat16)


def rotary_parts(key):
    base_key = jax.random.fold_in(key, 404)
    cache_key, query_key = jax.random.split(base_key, 2)
    cached = jax.random.truncated_normal(cache_key, -4.5, 4.5, (REQS, ROPE, MAX_LEN), jnp.float32)
    queries = jax.random.truncated_normal(query_key, -4.5, 4.5, (REQS, HEADS, ROPE), jnp.float32)
    return (queries, cached)


def draw_query_rotary(key, part):
    queries, cached = rotary_parts(key)
    return queries.astype(jnp.bfloat16)


def draw_rotary_cache(key, part):
    queries, cached = rotary_parts(key)
    return cached.astype(jnp.bfloat16)


def draw_lengths(key, part):
    base_key = jax.random.fold_in(key, 505)
    length_key, chosen_key = jax.random.split(base_key)
    drawn = jax.random.randint(length_key, (REQS,), 2, MAX_LEN + 1)
    chosen = jax.random.randint(chosen_key, (), 0, REQS)
    return jnp.where(jnp.arange(REQS) == chosen, MAX_LEN, drawn).astype(jnp.int32)


def level_of(own_key, dims, pieces, low, high):
    def one(axis_at, shards_of):
        steps = jax.random.uniform(jax.random.fold_in(jax.random.fold_in(own_key, 6), axis_at), (shards_of,), jnp.float32, low / len(pieces), high / len(pieces))
        return jnp.repeat(jnp.exp(steps), dims[axis_at] // shards_of).reshape((-1,) + (1,) * (len(dims) - axis_at - 1))

    loudness = one(*pieces[0])
    for cut in pieces[1:]:
        loudness = loudness * one(*cut)
    return loudness


def picks_of(key, rows, number_of, top, lift):
    sequence = jax.random.permutation(jax.random.fold_in(key, 1), number_of)
    boost = sequence
    for power in range(3):
        boost = boost * boost // number_of
    boost = boost * lift // number_of
    chance = jax.random.randint(jax.random.fold_in(key, 2), (rows, number_of), 0, 4096) + boost
    sure = jax.random.permutation(jax.random.fold_in(key, 3), rows)[jnp.arange(number_of) % rows]
    chance = jnp.where(jnp.arange(rows)[:, None] == sure[None, :], 1 << 14, chance)
    score = chance * number_of + jnp.arange(number_of)
    return lax.top_k(score.astype(jnp.int32), top)[1].astype(jnp.int32)


def bell_draw(stream_key, extent, deviation, limit, pieces=(), kind=jnp.bfloat16):
    values = jax.random.normal(stream_key, extent, jnp.float32) * deviation
    if len(pieces) > 0:
        values = level_of(stream_key, extent, pieces, -0.22, 0.18) * values
    return jnp.clip(values, min=-limit, max=limit).astype(kind)


def setup_inputs(seed: int = 0) -> dict:
    keys = jax.random.split(jax.random.key(seed), 21)
    residual = draw_residual(jax.random.fold_in(keys[20], 71), 0)
    query_plain = bell_draw(keys[1], (REQS, HEADS, NOPE), 1.0, 6.0, ((0, 4),))
    query_rotary = draw_query_rotary(jax.random.fold_in(keys[20], 71), 0)
    latent_cache = draw_latent_cache(jax.random.fold_in(keys[20], 71), 0)
    rotary_cache = draw_rotary_cache(jax.random.fold_in(keys[20], 71), 0)
    lengths = draw_lengths(jax.random.fold_in(keys[20], 71), 0)
    absorb_key = bell_draw(keys[6], (HEADS, NOPE, LATENT), NOPE ** -0.5, 0.5)
    absorb_value = bell_draw(keys[7], (HEADS, LATENT, VDIM), LATENT ** -0.5, 0.25)
    output_weight = bell_draw(keys[8], (HEADS * VDIM, D), (HEADS * VDIM) ** -0.5, 0.125, ((1, 32),))
    middle_gain = jnp.clip(1.0 + 0.1 * jax.random.normal(keys[9], (D,), jnp.float32), 0.5, 1.5)
    routes = picks_of(keys[10], REQS, EXPERTS, TOPK, 1536)
    route_weights = jnp.clip(jax.random.uniform(keys[11], (REQS, TOPK), jnp.float32, 0.05, 0.45), 0.05, 0.45)
    gate_weight = bell_draw(keys[12], (EXPERTS, D, FF_E), D ** -0.5, 0.125, ((0, 8), (2, 4)))
    up_weight = bell_draw(keys[13], (EXPERTS, D, FF_E), D ** -0.5, 0.125, ((0, 8), (2, 4)))
    down_weight = bell_draw(keys[14], (EXPERTS, FF_E, D), FF_E ** -0.5, 0.15625, ((0, 8), (1, 4)))
    shared_gate = bell_draw(keys[15], (D, SHARED_FF), D ** -0.5, 0.125, ((1, 32),))
    shared_up = bell_draw(keys[16], (D, SHARED_FF), D ** -0.5, 0.125, ((1, 32),))
    shared_down = bell_draw(keys[17], (SHARED_FF, D), SHARED_FF ** -0.5, 0.109375, ((0, 32),))
    final_gain = jnp.clip(1.0 + 0.1 * jax.random.normal(keys[18], (D,), jnp.float32), 0.5, 1.5)
    unembed = draw_unembed(jax.random.fold_in(keys[20], 71), 0)
    return {"residual": residual, "query_plain": query_plain, "query_rotary": query_rotary, "latent_cache": latent_cache, "rotary_cache": rotary_cache, "lengths": lengths, "absorb_key": absorb_key, "absorb_value": absorb_value, "output_weight": output_weight, "middle_gain": middle_gain, "routes": routes, "route_weights": route_weights, "gate_weight": gate_weight, "up_weight": up_weight, "down_weight": down_weight, "shared_gate": shared_gate, "shared_up": shared_up, "shared_down": shared_down, "final_gain": final_gain, "unembed": unembed}


NEG_FILL = -1e+30
NORM_EPS = 1e-06

def normed(hidden, gain):
    widened = hidden.astype(jnp.float32)
    meansq = lax.optimization_barrier(jnp.mean(widened * widened, axis=-1, keepdims=True))
    return (widened * lax.rsqrt(meansq + NORM_EPS) * gain).astype(jnp.bfloat16)

def attend(query_latent, query_rotary, latent_rows, rotary_rows, length):
    score_scale = (NOPE + ROPE) ** (-0.5)
    scores = jnp.dot(query_latent, latent_rows.T, preferred_element_type=jnp.float32)
    scores = (scores + jnp.dot(query_rotary, rotary_rows, preferred_element_type=jnp.float32)) * score_scale
    block_count = MAX_LEN // CTX_DEV
    scores = scores.reshape(HEADS, block_count, CTX_DEV)
    position = lax.broadcasted_iota(jnp.int32, (1, block_count, CTX_DEV), 1) * CTX_DEV + lax.broadcasted_iota(jnp.int32, (1, block_count, CTX_DEV), 2)
    usable = position < length
    block_peak = lax.optimization_barrier(jnp.max(jnp.where(usable, scores, NEG_FILL), axis=2))
    weights = jnp.where(usable, jnp.exp(scores - block_peak[:, :, None]), 0.0).astype(jnp.bfloat16)
    block_total = lax.optimization_barrier(jnp.sum(weights.astype(jnp.float32), axis=2))
    block_mix = jnp.einsum('hbt,btc->hbc', weights.astype(jnp.float32), latent_rows.reshape(block_count, CTX_DEV, LATENT).astype(jnp.float32), precision=lax.Precision.HIGHEST)
    largest = lax.optimization_barrier(jnp.max(block_peak, axis=1))
    rescale = jnp.exp(block_peak - largest[:, None])
    return lax.optimization_barrier(jnp.sum(rescale[:, :, None] * block_mix, axis=1)) / lax.optimization_barrier(jnp.sum(rescale * block_total, axis=1))[:, None]

def reference(residual, query_plain, query_rotary, latent_cache, rotary_cache, lengths, absorb_key, absorb_value, output_weight, middle_gain, routes, route_weights, gate_weight, up_weight, down_weight, shared_gate, shared_up, shared_down, final_gain, unembed):
    query_latent = jnp.einsum('rhn,hnc->rhc', query_plain.astype(jnp.float32), absorb_key.astype(jnp.float32), precision=lax.Precision.HIGHEST).astype(jnp.bfloat16)
    attn_latent = lax.map(lambda item: attend(item[0], item[1], item[2], item[3], item[4]), (query_latent, query_rotary, latent_cache, rotary_cache, lengths))
    heads_out = jnp.einsum('rhc,hcv->rhv', attn_latent, absorb_value.astype(jnp.float32), precision=lax.Precision.HIGHEST).astype(jnp.bfloat16)
    heads_out = heads_out.reshape(REQS, HEADS * VDIM)
    attn_out = jnp.dot(heads_out, output_weight, preferred_element_type=jnp.float32)
    stream = (residual.astype(jnp.float32) + attn_out).astype(jnp.bfloat16)
    expert_in = normed(stream, middle_gain)
    expert_range = jnp.arange(EXPERTS, dtype=jnp.int32)
    route_share = lax.optimization_barrier(jnp.sum(jnp.where(routes[:, :, None] == expert_range[None, None, :], route_weights[:, :, None], 0.0), axis=1))
    shared_gated = jnp.dot(expert_in, shared_gate, preferred_element_type=jnp.float32)
    shared_upper = jnp.dot(expert_in, shared_up, preferred_element_type=jnp.float32)
    shared_act = (jax.nn.silu(shared_gated) * shared_upper).astype(jnp.bfloat16)
    shared_term = jnp.dot(shared_act, shared_down, preferred_element_type=jnp.float32)

    def expert_step(carry, item):
        gate_rows, up_rows, down_rows, share = item
        gate = jnp.dot(expert_in, gate_rows, preferred_element_type=jnp.float32)
        upper = jnp.dot(expert_in, up_rows, preferred_element_type=jnp.float32)
        expert_act = (jax.nn.silu(gate) * upper).astype(jnp.bfloat16)
        return (carry + share[:, None] * jnp.dot(expert_act, down_rows, preferred_element_type=jnp.float32), None)
    moe, unused = lax.scan(expert_step, shared_term, (gate_weight, up_weight, down_weight, route_share.T))
    layer_out = (stream.astype(jnp.float32) + moe).astype(jnp.bfloat16)
    final_in = normed(layer_out, final_gain)
    logits = jnp.dot(final_in, unembed.T, preferred_element_type=jnp.float32)
    best_logits = lax.top_k(logits, 2)[0]
    return (layer_out, best_logits)
```

```python
import functools
import jax
import jax.numpy as jnp
from jax import lax
from jax.experimental import pallas as pl
from jax.experimental.pallas import tpu as pltpu
from jax.sharding import PartitionSpec as P

NEG_FILL = -1e30
NORM_EPS = 1e-06


def combined_all(x, axis, join):
    gathered = jax.tree.map(
        lambda a, kind: lax.all_gather(a.astype(kind), axis),
        x,
        (jnp.bfloat16, jnp.bfloat16, jnp.bfloat16),
    )

    def take(source):
        return jax.tree.map(
            lambda a, own: lax.dynamic_index_in_dim(a, source, 0, False).astype(own.dtype),
            gathered,
            x,
        )

    return lax.fori_loop(
        1, lax.axis_size(axis), lambda source, state: join(state, take(source)), take(0)
    )


def merged_2(x, axis, combine):
    everything = lax.all_gather(x, axis)
    first = everything[0]

    def hop(k, so_far):
        return combine(so_far, everything[k])

    return lax.fori_loop(1, lax.axis_size(axis), hop, first)


def normed(hidden, gain):
    widened = hidden.astype(jnp.float32)
    meansq = jnp.mean(widened * widened, axis=-1, keepdims=True)
    return (widened * lax.rsqrt(meansq + NORM_EPS) * gain).astype(jnp.bfloat16)


def blend(former, latter):
    largest = jnp.maximum(former[0], latter[0])
    former_rescale = jnp.exp(former[0] - largest)
    latter_rescale = jnp.exp(latter[0] - largest)
    totals = former_rescale * former[1] + latter_rescale * latter[1]
    mixes = former_rescale[..., None] * former[2] + latter_rescale[..., None] * latter[2]
    return (largest, totals, mixes)


def best_two(former, latter):
    higher = jnp.maximum(former[:, 0], latter[:, 0])
    lower = jnp.maximum(
        jnp.minimum(former[:, 0], latter[:, 0]), jnp.maximum(former[:, 1], latter[:, 1])
    )
    return jnp.stack([higher, lower], axis=1)


def local(
    residual,
    query_plain,
    query_rotary,
    latent_cache,
    rotary_cache,
    lengths,
    absorb_key,
    absorb_value,
    output_weight,
    middle_gain,
    routes,
    route_weights,
    gate_weight,
    up_weight,
    down_weight,
    shared_gate,
    shared_up,
    shared_down,
    final_gain,
    unembed,
):
    group_rows, head_count, plain_size = query_plain.shape
    block_len = latent_cache.shape[1]
    value_size = absorb_value.shape[2]
    score_scale = (plain_size + query_rotary.shape[2]) ** (-0.5)
    value_wide = absorb_value.astype(jnp.float32)
    query_latent = jnp.einsum(
        "rhn,hnc->rhc", query_plain, absorb_key, preferred_element_type=jnp.float32
    ).astype(jnp.bfloat16)
    scores = jnp.einsum(
        "rhc,rtc->rht", query_latent, latent_cache, preferred_element_type=jnp.float32
    )
    scores = (
        scores
        + jnp.einsum("rhj,rjt->rht", query_rotary, rotary_cache, preferred_element_type=jnp.float32)
    ) * score_scale
    position = lax.axis_index("seq") * block_len + lax.broadcasted_iota(
        jnp.int32, (1, 1, block_len), 2
    )
    usable = position < lengths[:, None, None]
    block_peak = jnp.max(jnp.where(usable, scores, NEG_FILL), axis=2)
    weights = jnp.where(usable, jnp.exp(scores - block_peak[:, :, None]), 0.0).astype(jnp.bfloat16)
    block_total = jnp.sum(weights.astype(jnp.float32), axis=2)
    block_mix = jnp.einsum(
        "rht,rtc->rhc", weights, latent_cache, preferred_element_type=jnp.float32
    )
    merged_peak, merged_total, merged_mix = combined_all(
        (block_peak, block_total, block_mix), "seq", blend
    )
    merged = merged_mix / merged_total[:, :, None]
    merged = jnp.einsum("rhc,hcv->rhv", merged, value_wide, precision=lax.Precision.HIGHEST)
    group_output = merged.astype(jnp.bfloat16).reshape(group_rows, head_count * value_size)
    attn_out = jnp.dot(
        lax.all_gather(group_output, "req", axis=0, tiled=True),
        output_weight,
        preferred_element_type=jnp.float32,
    )
    column_count = residual.shape[1]
    stream_cols = (residual.astype(jnp.float32) + attn_out).astype(jnp.bfloat16)
    stream = lax.all_gather(stream_cols, ("req", "seq"), axis=1, tiled=True)
    expert_in = normed(stream, middle_gain)
    local_count = gate_weight.shape[0]
    expert_index = lax.axis_index("seq") * local_count + lax.broadcasted_iota(
        jnp.int32, (local_count, 1, 1), 0
    )
    route_share = jnp.sum(
        jnp.where(routes[None, :, :] == expert_index, route_weights[None, :, :], 0.0), axis=2
    )
    gate = jnp.einsum("td,edf->etf", expert_in, gate_weight, preferred_element_type=jnp.float32)
    upper = jnp.einsum("td,edf->etf", expert_in, up_weight, preferred_element_type=jnp.float32)
    expert_act = (jax.nn.silu(gate) * upper).astype(jnp.bfloat16)
    expert_back = jnp.einsum(
        "etf,efd->etd", expert_act, down_weight, preferred_element_type=jnp.float32
    )
    shared_gated = jnp.dot(expert_in, shared_gate, preferred_element_type=jnp.float32)
    shared_upper = jnp.dot(expert_in, shared_up, preferred_element_type=jnp.float32)
    shared_act = (jax.nn.silu(shared_gated) * shared_upper).astype(jnp.bfloat16)
    shared_back = jnp.dot(shared_act, shared_down, preferred_element_type=jnp.float32)
    expert_term = jnp.sum(route_share[:, :, None] * expert_back, axis=0) + shared_back
    column_start = lax.axis_index(("req", "seq")) * column_count
    moe = lax.psum(expert_term, ("req", "seq"))
    layer_full = (stream.astype(jnp.float32) + moe).astype(jnp.bfloat16)
    layer_out = lax.dynamic_slice_in_dim(layer_full, column_start, column_count, 1)
    final_in = normed(layer_full, final_gain)
    logits = lax.dot_general(
        final_in, unembed, (((1,), (1,)), ((), ())), preferred_element_type=jnp.float32
    )
    local_best = lax.top_k(logits, 2)[0]
    best_logits = merged_2(local_best, ("req", "seq"), best_two)
    return (layer_out, best_logits)


NT = (((1,), (1,)), ((), ()))
SLOTS = 4
VOCAB_PIECES = 5
MESH = pl.DeviceIdType.MESH


def layer_kernel(
    n_req,
    n_seq,
    plain_size,
    lengths_ref,
    query_latent_ref,
    query_rotary_ref,
    residual_ref,
    routes_ref,
    route_weights_ref,
    middle_gain_ref,
    final_gain_ref,
    latent_hbm,
    rotary_hbm,
    value_hbm,
    output_hbm,
    gate_hbm,
    up_hbm,
    down_hbm,
    shared_gate_hbm,
    shared_up_hbm,
    shared_down_hbm,
    unembed_hbm,
    layer_ref,
    best_ref,
    latent_buf,
    rotary_buf,
    value_buf,
    output_buf,
    residual_buf,
    gate_buf,
    up_buf,
    down_buf,
    shared_gate_buf,
    shared_up_buf,
    shared_down_buf,
    unembed_buf,
    stage,
    mix_send,
    mix_recv,
    heads_send,
    heads_full,
    stream_full,
    normed_buf,
    moe_acc,
    moe_send,
    moe_recv,
    layer_full,
    best_send,
    best_recv,
    latent_sem,
    local_sem,
    expert_sem,
    unembed_sem,
    pair_sem,
    mix_sem,
    heads_sem,
    stream_sem,
    moe_sem,
    layer_sem,
    best_sem,
):
    n_dev = n_req * n_seq
    n_pair = n_dev // 2
    rows, heads, latent = query_latent_ref.shape
    block_len = latent_hbm.shape[1]
    experts = gate_hbm.shape[0]
    tokens, width = stream_full.shape
    half = tokens // 2
    own_heads = heads // n_seq
    mix_rows = own_heads * rows
    chunks = latent // 128
    score_scale = (plain_size + query_rotary_ref.shape[2]) ** (-0.5)
    req = lax.axis_index("req")
    seq = lax.axis_index("seq")
    me = req * n_seq + seq
    core = lax.rem(seq, 2)
    pair = lax.div(me, 2)

    def place(d):
        return (lax.div(d, n_seq), lax.rem(d, n_seq))

    barrier = pltpu.get_barrier_semaphore()

    @pl.loop(1, n_dev)
    def _(k):
        pl.semaphore_signal(
            barrier, inc=1, device_id=place(lax.rem(me + k, n_dev)), device_id_type=MESH
        )

    def latent_copy(i):
        slot = lax.rem(i, SLOTS)
        return pltpu.make_async_copy(latent_hbm.at[i], latent_buf.at[slot], latent_sem.at[slot])

    my_output_rows = pl.ds(pl.multiple_of(core * 64, 64), 64)
    local_copies = [
        pltpu.make_async_copy(rotary_hbm, rotary_buf, local_sem.at[0]),
        pltpu.make_async_copy(
            value_hbm.at[pl.ds(seq * own_heads, own_heads)], value_buf, local_sem.at[1]
        ),
        pltpu.make_async_copy(output_hbm, output_buf.at[my_output_rows], local_sem.at[2]),
        pltpu.make_async_copy(shared_gate_hbm, shared_gate_buf, local_sem.at[3]),
        pltpu.make_async_copy(shared_up_hbm, shared_up_buf, local_sem.at[4]),
        pltpu.make_async_copy(shared_down_hbm, shared_down_buf, local_sem.at[5]),
    ]

    def expert_copy(which, e):
        source, target = ((gate_hbm, gate_buf), (up_hbm, up_buf), (down_hbm, down_buf))[which]
        return pltpu.make_async_copy(source.at[e], target.at[e], expert_sem.at[which, e])

    piece = unembed_hbm.shape[0] // VOCAB_PIECES

    def unembed_copy(v):
        place_rows = pl.ds(pl.multiple_of(v * piece, 64), piece)
        return pltpu.make_async_copy(
            unembed_hbm.at[place_rows], unembed_buf.at[place_rows], unembed_sem.at[v]
        )

    local_copies[0].start()
    for i in range(SLOTS):
        latent_copy(i).start()
    for copy in local_copies[1:]:
        copy.start()
    local_copies[0].wait()
    residual_buf[core] = residual_ref[...]

    lane = lax.broadcasted_iota(jnp.int32, (heads, 128), 1)
    position = seq * block_len + lax.broadcasted_iota(jnp.int32, (heads, block_len), 1)

    @pl.loop(0, rows)
    def _(i):
        slot = lax.rem(i, SLOTS)
        latent_copy(i).wait()
        cached = latent_buf[slot]
        scores = lax.dot_general(
            query_latent_ref[i], cached, NT, preferred_element_type=jnp.float32
        )
        scores = (
            scores
            + jnp.dot(query_rotary_ref[i], rotary_buf[i], preferred_element_type=jnp.float32)
        ) * score_scale
        usable = position < lengths_ref[i]
        peak = jnp.max(jnp.where(usable, scores, NEG_FILL), axis=1, keepdims=True)
        weights = jnp.where(usable, jnp.exp(scores - peak), 0.0).astype(jnp.bfloat16)
        total = jnp.sum(weights.astype(jnp.float32), axis=1, keepdims=True)
        mix = jnp.dot(weights, cached, preferred_element_type=jnp.float32)
        for c in range(chunks):
            stage[c, pl.ds(i, heads, stride=rows), :] = mix[:, c * 128 : (c + 1) * 128]
        info = jnp.zeros((heads, 128), jnp.float32)
        at = 0
        for value in (peak, total):
            rest = value
            for _ in range(3):
                part = rest.astype(jnp.bfloat16).astype(jnp.float32)
                info = jnp.where(lane == at, part, info)
                rest = rest - part
                at += 1
        stage[chunks, pl.ds(i, heads, stride=rows), :] = info

        @pl.when(i + SLOTS < rows)
        def _():
            latent_copy(i + SLOTS).start()

        @pl.when(i < experts)
        def _():
            expert_copy(0, i).start()
            expert_copy(1, i).start()
            expert_copy(2, i).start()

    for v in range(VOCAB_PIECES):
        unembed_copy(v).start()

    pl.semaphore_wait(barrier, n_dev - 1)

    def mix_copy(k):
        other = lax.rem(seq + k, n_seq)
        source = lax.rem(seq + n_seq - k, n_seq)
        sent = pltpu.make_async_remote_copy(
            src_ref=mix_send.at[other],
            dst_ref=mix_recv.at[seq],
            send_sem=mix_sem.at[0, k],
            recv_sem=mix_sem.at[1, seq],
            device_id=(req, other),
            device_id_type=MESH,
        )
        got = pltpu.make_async_remote_copy(
            src_ref=mix_send.at[other],
            dst_ref=mix_recv.at[source],
            send_sem=mix_sem.at[0, k],
            recv_sem=mix_sem.at[1, source],
            device_id=(req, other),
            device_id_type=MESH,
        )
        return sent, got

    @pl.loop(1, n_seq)
    def _(k):
        other = lax.rem(seq + k, n_seq)
        mine = pl.ds(pl.multiple_of(other * mix_rows, 16), mix_rows)
        mix_send[other] = stage[:, mine, :].astype(jnp.bfloat16)
        mix_copy(k)[0].start()

    mix_recv[seq] = stage[:, pl.ds(pl.multiple_of(seq * mix_rows, 16), mix_rows), :].astype(
        jnp.bfloat16
    )

    sibling = (req, seq + 1 - 2 * core)
    their_output_rows = pl.ds(pl.multiple_of((1 - core) * 64, 64), 64)

    def pair_copies(to_rows, to_slot):
        return (
            pltpu.make_async_remote_copy(
                src_ref=output_hbm,
                dst_ref=output_buf.at[to_rows],
                send_sem=pair_sem.at[0],
                recv_sem=pair_sem.at[1],
                device_id=sibling,
                device_id_type=MESH,
            ),
            pltpu.make_async_remote_copy(
                src_ref=residual_buf.at[core],
                dst_ref=residual_buf.at[to_slot],
                send_sem=pair_sem.at[2],
                recv_sem=pair_sem.at[3],
                device_id=sibling,
                device_id_type=MESH,
            ),
        )

    pair_sends = pair_copies(my_output_rows, core)
    pair_gets = pair_copies(their_output_rows, 1 - core)
    for copy in pair_sends:
        copy.start()

    @pl.loop(1, n_seq)
    def _(k):
        mix_copy(k)[1].wait_recv()

    info = mix_recv[:, chunks].astype(jnp.float32)
    info_lane = lax.broadcasted_iota(jnp.int32, info.shape, 2)
    peaks = jnp.sum(jnp.where(info_lane < 3, info, 0.0), axis=2, keepdims=True)
    totals = jnp.sum(
        jnp.where(info_lane < 3, 0.0, info), axis=2, keepdims=True
    )
    rescale = jnp.exp(peaks - jnp.max(peaks, axis=0, keepdims=True))
    denominator = jnp.sum(rescale * totals, axis=0)
    local_copies[1].wait()
    attended = jnp.concatenate(
        [
            jnp.sum(rescale * mix_recv[:, c].astype(jnp.float32), axis=0) / denominator
            for c in range(chunks)
        ],
        axis=1,
    )
    upper_part = attended.astype(jnp.bfloat16)
    lower_part = (attended - upper_part.astype(jnp.float32)).astype(jnp.bfloat16)
    value_size = value_buf.shape[2]
    for j in range(own_heads):
        span = slice(j * rows, (j + 1) * rows)
        made = jnp.dot(upper_part[span], value_buf[j], preferred_element_type=jnp.float32)
        made += jnp.dot(lower_part[span], value_buf[j], preferred_element_type=jnp.float32)
        heads_send[:, j * value_size : (j + 1) * value_size] = made.astype(jnp.bfloat16)

    head_cols = own_heads * value_size
    wanted_core = lax.div(req, n_req // 2)
    in_half = n_req // 2

    def heads_slot(r, s):
        return heads_full.at[
            pl.ds(pl.multiple_of(lax.rem(r, in_half) * rows, rows), rows),
            pl.ds(pl.multiple_of(s * head_cols, 128), head_cols),
        ]

    def heads_copy(target, r, s):
        return pltpu.make_async_remote_copy(
            src_ref=heads_send,
            dst_ref=heads_slot(r, s),
            send_sem=heads_sem.at[0, lax.div(target, 2)],
            recv_sem=heads_sem.at[1, lax.rem(r, in_half) * n_seq + s],
            device_id=place(target),
            device_id_type=MESH,
        )

    @pl.loop(0, n_pair)
    def _(k):
        target = lax.rem(pair + 1 + k, n_pair) * 2 + wanted_core

        @pl.when(target != me)
        def _():
            heads_copy(target, req, seq).start()

    @pl.when(core == wanted_core)
    def _():
        heads_slot(req, seq)[...] = heads_send[...]

    for copy in pair_gets:
        copy.wait_recv()
    local_copies[2].wait()

    @pl.loop(0, n_pair)
    def _(k):
        r = core * in_half + lax.div(k, n_seq)
        s = lax.rem(k, n_seq)

        @pl.when(r * n_seq + s != me)
        def _():
            heads_copy(core, r, s).wait_recv()

    my_rows = pl.ds(pl.multiple_of(core * half, half), half)
    my_cols = pl.ds(pl.multiple_of(pair * 128, 128), 128)
    attn_out = lax.dot_general(
        heads_full[...], output_buf[...], NT, preferred_element_type=jnp.float32
    )
    entering = jnp.concatenate(
        [residual_buf[0, my_rows, :], residual_buf[1, my_rows, :]], axis=1
    ).astype(jnp.float32)
    stream_full[my_rows, my_cols] = (entering + attn_out).astype(jnp.bfloat16)

    def block_of(ref, d):
        return ref.at[
            pl.ds(pl.multiple_of(lax.rem(d, 2) * half, half), half),
            pl.ds(pl.multiple_of(lax.div(d, 2) * 128, 128), 128),
        ]

    def spread_copy(ref, sem, k, owner):
        return pltpu.make_async_remote_copy(
            src_ref=block_of(ref, owner),
            dst_ref=block_of(ref, owner),
            send_sem=sem.at[0, k],
            recv_sem=sem.at[1, owner],
            device_id=place(lax.rem(me + k, n_dev)),
            device_id_type=MESH,
        )

    def spread(ref, sem):
        @pl.loop(1, n_dev)
        def _(k):
            spread_copy(ref, sem, k, me).start()

    def collect(ref, sem):
        @pl.loop(1, n_dev)
        def _(k):
            spread_copy(ref, sem, k, lax.rem(me + n_dev - k, n_dev)).wait_recv()

    spread(stream_full, stream_sem)
    for copy in local_copies[3:]:
        copy.wait()
    collect(stream_full, stream_sem)
    normed_buf[...] = normed(stream_full[...], middle_gain_ref[...])

    def glu(gate_rows, up_rows):
        hidden = normed_buf[...]
        gate = lax.dot_general(hidden, gate_rows, NT, preferred_element_type=jnp.float32)
        upper = lax.dot_general(hidden, up_rows, NT, preferred_element_type=jnp.float32)
        return (gate / (1.0 + jnp.exp(-gate)) * upper).astype(jnp.bfloat16)

    spans = [slice(c * 512, (c + 1) * 512) for c in range(width // 512)]
    shared_act = glu(shared_gate_buf[...], shared_up_buf[...])
    for span in spans:
        moe_acc[:, span] = jnp.dot(
            shared_act, shared_down_buf[:, span], preferred_element_type=jnp.float32
        )

    @pl.loop(0, experts)
    def _(e):
        for which in range(3):
            expert_copy(which, e).wait()
        share = jnp.sum(
            jnp.where(routes_ref[...] == seq * experts + e, route_weights_ref[...], 0.0),
            axis=1,
            keepdims=True,
        )
        act = glu(gate_buf[e], up_buf[e])
        for span in spans:
            moe_acc[:, span] += share * jnp.dot(
                act, down_buf[e, :, span], preferred_element_type=jnp.float32
            )

    moe_send[...] = moe_acc[...].astype(jnp.bfloat16)

    def moe_copy(k, owner):
        target = lax.rem(me + k, n_dev)
        return pltpu.make_async_remote_copy(
            src_ref=block_of(moe_send, target),
            dst_ref=moe_recv.at[owner],
            send_sem=moe_sem.at[0, k],
            recv_sem=moe_sem.at[1, owner],
            device_id=place(target),
            device_id_type=MESH,
        )

    @pl.loop(1, n_dev)
    def _(k):
        moe_copy(k, me).start()

    moe_recv[me] = moe_send[my_rows, my_cols]

    @pl.loop(1, n_dev)
    def _(k):
        moe_copy(k, lax.rem(me + n_dev - k, n_dev)).wait_recv()

    moe = jnp.sum(moe_recv[...].astype(jnp.float32), axis=0)
    layer_full[my_rows, my_cols] = (
        stream_full[my_rows, my_cols].astype(jnp.float32) + moe
    ).astype(jnp.bfloat16)
    spread(layer_full, layer_sem)
    collect(layer_full, layer_sem)
    shown = layer_full[:, my_cols].astype(jnp.float32)
    layer_ref[...] = jnp.where(core == 0, shown[:, :64], shown[:, 64:]).astype(jnp.bfloat16)
    normed_buf[...] = normed(layer_full[...], final_gain_ref[...])

    lowest = jnp.full((tokens, 128), -jnp.inf, jnp.float32)

    def vocab_step(v, state):
        first, second = state
        unembed_copy(v).wait()
        logits = lax.dot_general(
            normed_buf[...],
            unembed_buf[pl.ds(pl.multiple_of(v * piece, 64), piece), :],
            NT,
            preferred_element_type=jnp.float32,
        )
        for c in range(piece // 128):
            part = logits[:, c * 128 : (c + 1) * 128]
            second = jnp.maximum(second, jnp.minimum(first, part))
            first = jnp.maximum(first, part)
        return first, second

    first, second = lax.fori_loop(0, VOCAB_PIECES, vocab_step, (lowest, lowest))
    token_lane = lax.broadcasted_iota(jnp.int32, (tokens, 128), 1)
    top = jnp.max(first, axis=1, keepdims=True)
    where_top = jnp.min(
        jnp.where(first == top, token_lane, 128), axis=1, keepdims=True
    )
    runner = jnp.max(
        jnp.where(token_lane == where_top, second, first), axis=1, keepdims=True
    )
    packed = jnp.where(token_lane == 0, top, runner)
    packed = jnp.concatenate([packed, packed], axis=0).T
    best_send[...] = packed[:8]
    best_recv[me] = packed[:8]

    def best_copy(k, owner):
        return pltpu.make_async_remote_copy(
            src_ref=best_send,
            dst_ref=best_recv.at[owner],
            send_sem=best_sem.at[0, k],
            recv_sem=best_sem.at[1, owner],
            device_id=place(lax.rem(me + k, n_dev)),
            device_id_type=MESH,
        )

    @pl.loop(1, n_dev)
    def _(k):
        best_copy(k, me).start()

    for copy in pair_sends:
        copy.wait_send()

    @pl.loop(1, n_seq)
    def _(k):
        mix_copy(k)[0].wait_send()

    @pl.loop(0, n_pair)
    def _(k):
        target = k * 2 + wanted_core

        @pl.when(target != me)
        def _():
            heads_copy(target, req, seq).wait_send()

    @pl.loop(1, n_dev)
    def _(k):
        spread_copy(stream_full, stream_sem, k, me).wait_send()
        moe_copy(k, me).wait_send()
        spread_copy(layer_full, layer_sem, k, me).wait_send()

    @pl.loop(1, n_dev)
    def _(k):
        best_copy(k, lax.rem(me + n_dev - k, n_dev)).wait_recv()

    found = [best_recv[d] for d in range(n_dev)]
    pairs = [(x[0:1], x[1:2]) for x in found]
    while len(pairs) > 1:
        joined = [
            (
                jnp.maximum(a[0], b[0]),
                jnp.maximum(jnp.minimum(a[0], b[0]), jnp.maximum(a[1], b[1])),
            )
            for a, b in zip(pairs[0::2], pairs[1::2])
        ]
        pairs = joined
    best_ref[0:1, :] = pairs[0][0][:, :tokens]
    best_ref[1:2, :] = pairs[0][1][:, :tokens]

    @pl.loop(1, n_dev)
    def _(k):
        best_copy(k, me).wait_send()


def fits(n_req, n_seq, shapes):
    residual, query, cache, unembed = shapes
    return (
        n_req % 2 == 0
        and n_seq % 2 == 0
        and query[1] % n_seq == 0
        and query[0] % 16 == 0
        and residual[1] == 64
        and residual[0] == 64
        and cache[1] % 128 == 0
        and unembed[0] % (128 * VOCAB_PIECES) == 0
        and n_req * n_seq & (n_req * n_seq - 1) == 0
    )


def fused(
    n_req,
    n_seq,
    residual,
    query_plain,
    query_rotary,
    latent_cache,
    rotary_cache,
    lengths,
    absorb_key,
    absorb_value,
    output_weight,
    middle_gain,
    routes,
    route_weights,
    gate_weight,
    up_weight,
    down_weight,
    shared_gate,
    shared_up,
    shared_down,
    final_gain,
    unembed,
):
    query_latent = jnp.einsum(
        "rhn,hnc->rhc", query_plain, absorb_key, preferred_element_type=jnp.float32
    ).astype(jnp.bfloat16)
    rows, heads, latent = query_latent.shape
    tokens = residual.shape[0]
    width = unembed.shape[1]
    n_dev = n_req * n_seq
    block_len = latent_cache.shape[1]
    experts, ff = gate_weight.shape[0], gate_weight.shape[2]
    shared_ff = shared_gate.shape[1]
    own_heads = heads // n_seq
    value_size = absorb_value.shape[2]
    parts = latent // 128 + 1
    bf, f32 = jnp.bfloat16, jnp.float32
    dma = pltpu.SemaphoreType.DMA
    vmem = pl.BlockSpec(memory_space=pltpu.VMEM)
    anywhere = pl.BlockSpec(memory_space=pl.ANY)
    layer_out, best = pl.pallas_call(
        functools.partial(layer_kernel, n_req, n_seq, query_plain.shape[2]),
        name="layer",
        out_shape=(
            jax.ShapeDtypeStruct(residual.shape, bf),
            jax.ShapeDtypeStruct((2, tokens), f32),
        ),
        in_specs=[pl.BlockSpec(memory_space=pltpu.SMEM)] + [vmem] * 7 + [anywhere] * 11,
        out_specs=(vmem, vmem),
        scratch_shapes=[
            pltpu.VMEM((SLOTS, block_len, latent), bf),
            pltpu.VMEM(rotary_cache.shape, bf),
            pltpu.VMEM((own_heads, latent, value_size), bf),
            pltpu.VMEM((128, width), bf),
            pltpu.VMEM((2, tokens, 64), bf),
            pltpu.VMEM((experts, ff, width), bf),
            pltpu.VMEM((experts, ff, width), bf),
            pltpu.VMEM((experts, ff, width), bf),
            pltpu.VMEM((shared_ff, width), bf),
            pltpu.VMEM((shared_ff, width), bf),
            pltpu.VMEM((shared_ff, width), bf),
            pltpu.VMEM(unembed.shape, bf),
            pltpu.VMEM((parts, heads * rows, 128), f32),
            pltpu.VMEM((n_seq, parts, own_heads * rows, 128), bf),
            pltpu.VMEM((n_seq, parts, own_heads * rows, 128), bf),
            pltpu.VMEM((rows, own_heads * value_size), bf),
            pltpu.VMEM((tokens // 2, heads * value_size), bf),
            pltpu.VMEM((tokens, width), bf),
            pltpu.VMEM((tokens, width), bf),
            pltpu.VMEM((tokens, width), f32),
            pltpu.VMEM((tokens, width), bf),
            pltpu.VMEM((n_dev, tokens // 2, 128), bf),
            pltpu.VMEM((tokens, width), bf),
            pltpu.VMEM((8, 128), f32),
            pltpu.VMEM((n_dev, 8, 128), f32),
            dma((SLOTS,)),
            dma((6,)),
            dma((3, experts)),
            dma((VOCAB_PIECES,)),
            dma((4,)),
            dma((2, n_seq)),
            dma((2, n_dev // 2)),
            dma((2, n_dev)),
            dma((2, n_dev)),
            dma((2, n_dev)),
            dma((2, n_dev)),
        ],
        compiler_params=pltpu.CompilerParams(
            collective_id=0, has_side_effects=True, vmem_limit_bytes=63 * 1024 * 1024
        ),
    )(
        lengths,
        query_latent,
        query_rotary,
        residual,
        routes,
        route_weights,
        middle_gain.reshape(1, width),
        final_gain.reshape(1, width),
        latent_cache,
        rotary_cache,
        absorb_value,
        output_weight.T,
        jnp.swapaxes(gate_weight, 1, 2),
        jnp.swapaxes(up_weight, 1, 2),
        down_weight,
        shared_gate.T,
        shared_up.T,
        shared_down,
        unembed,
    )
    return layer_out, best.T


def chosen(n_req, n_seq, *args):
    shapes = (args[0].shape, args[1].shape, args[3].shape, args[19].shape)
    if fits(n_req, n_seq, shapes):
        return fused(n_req, n_seq, *args)
    return local(*args)


def solution(mesh):
    in_specs = (
        P(None, ("req", "seq")),
        P("req", None, None),
        P("req", None, None),
        P("req", "seq", None),
        P("req", None, "seq"),
        P("req"),
        P(),
        P(),
        P(None, ("req", "seq")),
        P(),
        P(),
        P(),
        P("seq", None, "req"),
        P("seq", None, "req"),
        P("seq", "req", None),
        P(None, ("req", "seq")),
        P(None, ("req", "seq")),
        P(("req", "seq"), None),
        P(),
        P(("req", "seq"), None),
    )
    out_specs = (P(None, ("req", "seq")), P())
    body = functools.partial(chosen, mesh.shape["req"], mesh.shape["seq"])
    return jax.shard_map(body, mesh=mesh, in_specs=in_specs, out_specs=out_specs, check_vma=False)
```

```python
import functools
import jax
import jax.numpy as jnp
from jax import lax
from jax.experimental import pallas as pl
from jax.experimental.pallas import tpu as pltpu
from jax.sharding import PartitionSpec as P

NEG_FILL = -1e30
NORM_EPS = 1e-06


def combined_all(x, axis, join):
    gathered = jax.tree.map(
        lambda a, kind: lax.all_gather(a.astype(kind), axis),
        x,
        (jnp.bfloat16, jnp.bfloat16, jnp.bfloat16),
    )

    def take(source):
        return jax.tree.map(
            lambda a, own: lax.dynamic_index_in_dim(a, source, 0, False).astype(own.dtype),
            gathered,
            x,
        )

    return lax.fori_loop(
        1, lax.axis_size(axis), lambda source, state: join(state, take(source)), take(0)
    )


def merged_2(x, axis, combine):
    everything = lax.all_gather(x, axis)
    first = everything[0]

    def hop(k, so_far):
        return combine(so_far, everything[k])

    return lax.fori_loop(1, lax.axis_size(axis), hop, first)


def normed(hidden, gain):
    widened = hidden.astype(jnp.float32)
    meansq = jnp.mean(widened * widened, axis=-1, keepdims=True)
    return (widened * lax.rsqrt(meansq + NORM_EPS) * gain).astype(jnp.bfloat16)


def blend(former, latter):
    largest = jnp.maximum(former[0], latter[0])
    former_rescale = jnp.exp(former[0] - largest)
    latter_rescale = jnp.exp(latter[0] - largest)
    totals = former_rescale * former[1] + latter_rescale * latter[1]
    mixes = former_rescale[..., None] * former[2] + latter_rescale[..., None] * latter[2]
    return (largest, totals, mixes)


def best_two(former, latter):
    higher = jnp.maximum(former[:, 0], latter[:, 0])
    lower = jnp.maximum(
        jnp.minimum(former[:, 0], latter[:, 0]), jnp.maximum(former[:, 1], latter[:, 1])
    )
    return jnp.stack([higher, lower], axis=1)


def local(
    residual,
    query_plain,
    query_rotary,
    latent_cache,
    rotary_cache,
    lengths,
    absorb_key,
    absorb_value,
    output_weight,
    middle_gain,
    routes,
    route_weights,
    gate_weight,
    up_weight,
    down_weight,
    shared_gate,
    shared_up,
    shared_down,
    final_gain,
    unembed,
):
    group_rows, head_count, plain_size = query_plain.shape
    block_len = latent_cache.shape[1]
    value_size = absorb_value.shape[2]
    score_scale = (plain_size + query_rotary.shape[2]) ** (-0.5)
    value_wide = absorb_value.astype(jnp.float32)
    query_latent = jnp.einsum(
        "rhn,hnc->rhc", query_plain, absorb_key, preferred_element_type=jnp.float32
    ).astype(jnp.bfloat16)
    scores = jnp.einsum(
        "rhc,rtc->rht", query_latent, latent_cache, preferred_element_type=jnp.float32
    )
    scores = (
        scores
        + jnp.einsum("rhj,rjt->rht", query_rotary, rotary_cache, preferred_element_type=jnp.float32)
    ) * score_scale
    position = lax.axis_index("seq") * block_len + lax.broadcasted_iota(
        jnp.int32, (1, 1, block_len), 2
    )
    usable = position < lengths[:, None, None]
    block_peak = jnp.max(jnp.where(usable, scores, NEG_FILL), axis=2)
    weights = jnp.where(usable, jnp.exp(scores - block_peak[:, :, None]), 0.0).astype(jnp.bfloat16)
    block_total = jnp.sum(weights.astype(jnp.float32), axis=2)
    block_mix = jnp.einsum(
        "rht,rtc->rhc", weights, latent_cache, preferred_element_type=jnp.float32
    )
    merged_peak, merged_total, merged_mix = combined_all(
        (block_peak, block_total, block_mix), "seq", blend
    )
    merged = merged_mix / merged_total[:, :, None]
    merged = jnp.einsum("rhc,hcv->rhv", merged, value_wide, precision=lax.Precision.HIGHEST)
    group_output = merged.astype(jnp.bfloat16).reshape(group_rows, head_count * value_size)
    attn_out = jnp.dot(
        lax.all_gather(group_output, "req", axis=0, tiled=True),
        output_weight,
        preferred_element_type=jnp.float32,
    )
    column_count = residual.shape[1]
    stream_cols = (residual.astype(jnp.float32) + attn_out).astype(jnp.bfloat16)
    stream = lax.all_gather(stream_cols, ("req", "seq"), axis=1, tiled=True)
    expert_in = normed(stream, middle_gain)
    local_count = gate_weight.shape[0]
    expert_index = lax.axis_index("seq") * local_count + lax.broadcasted_iota(
        jnp.int32, (local_count, 1, 1), 0
    )
    route_share = jnp.sum(
        jnp.where(routes[None, :, :] == expert_index, route_weights[None, :, :], 0.0), axis=2
    )
    gate = jnp.einsum("td,edf->etf", expert_in, gate_weight, preferred_element_type=jnp.float32)
    upper = jnp.einsum("td,edf->etf", expert_in, up_weight, preferred_element_type=jnp.float32)
    expert_act = (jax.nn.silu(gate) * upper).astype(jnp.bfloat16)
    expert_back = jnp.einsum(
        "etf,efd->etd", expert_act, down_weight, preferred_element_type=jnp.float32
    )
    shared_gated = jnp.dot(expert_in, shared_gate, preferred_element_type=jnp.float32)
    shared_upper = jnp.dot(expert_in, shared_up, preferred_element_type=jnp.float32)
    shared_act = (jax.nn.silu(shared_gated) * shared_upper).astype(jnp.bfloat16)
    shared_back = jnp.dot(shared_act, shared_down, preferred_element_type=jnp.float32)
    expert_term = jnp.sum(route_share[:, :, None] * expert_back, axis=0) + shared_back
    column_start = lax.axis_index(("req", "seq")) * column_count
    moe = lax.psum(expert_term, ("req", "seq"))
    layer_full = (stream.astype(jnp.float32) + moe).astype(jnp.bfloat16)
    layer_out = lax.dynamic_slice_in_dim(layer_full, column_start, column_count, 1)
    final_in = normed(layer_full, final_gain)
    logits = lax.dot_general(
        final_in, unembed, (((1,), (1,)), ((), ())), preferred_element_type=jnp.float32
    )
    local_best = lax.top_k(logits, 2)[0]
    best_logits = merged_2(local_best, ("req", "seq"), best_two)
    return (layer_out, best_logits)


NT = (((1,), (1,)), ((), ()))
SLOTS = 4
VOCAB_PIECES = 5
MESH = pl.DeviceIdType.MESH


def layer_kernel(
    n_req,
    n_seq,
    plain_size,
    lengths_ref,
    query_latent_ref,
    query_rotary_ref,
    residual_ref,
    routes_ref,
    route_weights_ref,
    middle_gain_ref,
    final_gain_ref,
    latent_hbm,
    rotary_hbm,
    value_hbm,
    output_hbm,
    gate_hbm,
    up_hbm,
    down_hbm,
    shared_gate_hbm,
    shared_up_hbm,
    shared_down_hbm,
    unembed_hbm,
    layer_ref,
    best_ref,
    latent_buf,
    rotary_buf,
    value_buf,
    output_buf,
    residual_buf,
    gate_buf,
    up_buf,
    down_buf,
    shared_gate_buf,
    shared_up_buf,
    shared_down_buf,
    unembed_buf,
    stage,
    mix_send,
    mix_recv,
    heads_send,
    heads_full,
    stream_full,
    normed_buf,
    moe_acc,
    moe_send,
    moe_theirs,
    moe_sums,
    moe_recv,
    layer_full,
    best_send,
    best_theirs,
    best_sums,
    best_recv,
    latent_sem,
    local_sem,
    expert_sem,
    unembed_sem,
    pair_sem,
    mix_sem,
    heads_sem,
    stream_sem,
    moe_sem,
    layer_sem,
    best_sem,
):
    n_dev = n_req * n_seq
    n_pair = n_dev // 2
    rows, heads, latent = query_latent_ref.shape
    block_len = latent_hbm.shape[1]
    experts = gate_hbm.shape[0]
    tokens, width = stream_full.shape
    half = tokens // 2
    own_heads = heads // n_seq
    mix_rows = own_heads * rows
    chunks = latent // 128
    score_scale = (plain_size + query_rotary_ref.shape[2]) ** (-0.5)
    req = lax.axis_index("req")
    seq = lax.axis_index("seq")
    me = req * n_seq + seq
    core = lax.rem(seq, 2)
    pair = lax.div(me, 2)

    def place(d):
        return (lax.div(d, n_seq), lax.rem(d, n_seq))

    barrier = pltpu.get_barrier_semaphore()

    @pl.loop(1, n_dev)
    def _(k):
        pl.semaphore_signal(
            barrier, inc=1, device_id=place(lax.rem(me + k, n_dev)), device_id_type=MESH
        )

    def latent_copy(i):
        slot = lax.rem(i, SLOTS)
        return pltpu.make_async_copy(latent_hbm.at[i], latent_buf.at[slot], latent_sem.at[slot])

    my_output_rows = pl.ds(pl.multiple_of(core * 64, 64), 64)
    local_copies = [
        pltpu.make_async_copy(rotary_hbm, rotary_buf, local_sem.at[0]),
        pltpu.make_async_copy(
            value_hbm.at[pl.ds(seq * own_heads, own_heads)], value_buf, local_sem.at[1]
        ),
        pltpu.make_async_copy(output_hbm, output_buf.at[my_output_rows], local_sem.at[2]),
        pltpu.make_async_copy(shared_gate_hbm, shared_gate_buf, local_sem.at[3]),
        pltpu.make_async_copy(shared_up_hbm, shared_up_buf, local_sem.at[4]),
        pltpu.make_async_copy(shared_down_hbm, shared_down_buf, local_sem.at[5]),
    ]

    def expert_copy(which, e):
        source, target = ((gate_hbm, gate_buf), (up_hbm, up_buf), (down_hbm, down_buf))[which]
        return pltpu.make_async_copy(source.at[e], target.at[e], expert_sem.at[which, e])

    piece = unembed_hbm.shape[0] // VOCAB_PIECES

    def unembed_copy(v):
        place_rows = pl.ds(pl.multiple_of(v * piece, 64), piece)
        return pltpu.make_async_copy(
            unembed_hbm.at[place_rows], unembed_buf.at[place_rows], unembed_sem.at[v]
        )

    local_copies[0].start()
    for i in range(SLOTS):
        latent_copy(i).start()
    for copy in local_copies[1:]:
        copy.start()
    local_copies[0].wait()
    residual_buf[core] = residual_ref[...]

    lane = lax.broadcasted_iota(jnp.int32, (heads, 128), 1)
    position = seq * block_len + lax.broadcasted_iota(jnp.int32, (heads, block_len), 1)

    @pl.loop(0, rows)
    def _(i):
        slot = lax.rem(i, SLOTS)
        latent_copy(i).wait()
        cached = latent_buf[slot]
        scores = lax.dot_general(
            query_latent_ref[i], cached, NT, preferred_element_type=jnp.float32
        )
        scores = (
            scores
            + jnp.dot(query_rotary_ref[i], rotary_buf[i], preferred_element_type=jnp.float32)
        ) * score_scale
        usable = position < lengths_ref[i]
        peak = jnp.max(jnp.where(usable, scores, NEG_FILL), axis=1, keepdims=True)
        weights = jnp.where(usable, jnp.exp(scores - peak), 0.0).astype(jnp.bfloat16)
        total = jnp.sum(weights.astype(jnp.float32), axis=1, keepdims=True)
        mix = jnp.dot(weights, cached, preferred_element_type=jnp.float32)
        for c in range(chunks):
            stage[c, pl.ds(i, heads, stride=rows), :] = mix[:, c * 128 : (c + 1) * 128]
        info = jnp.zeros((heads, 128), jnp.float32)
        at = 0
        for value in (peak, total):
            rest = value
            for _ in range(3):
                part = rest.astype(jnp.bfloat16).astype(jnp.float32)
                info = jnp.where(lane == at, part, info)
                rest = rest - part
                at += 1
        stage[chunks, pl.ds(i, heads, stride=rows), :] = info

        @pl.when(i + SLOTS < rows)
        def _():
            latent_copy(i + SLOTS).start()

        @pl.when(i < experts)
        def _():
            expert_copy(0, i).start()
            expert_copy(1, i).start()
            expert_copy(2, i).start()

    for v in range(VOCAB_PIECES):
        unembed_copy(v).start()

    pl.semaphore_wait(barrier, n_dev - 1)

    def mix_copy(k):
        other = lax.rem(seq + k, n_seq)
        source = lax.rem(seq + n_seq - k, n_seq)
        sent = pltpu.make_async_remote_copy(
            src_ref=mix_send.at[other],
            dst_ref=mix_recv.at[seq],
            send_sem=mix_sem.at[0, k],
            recv_sem=mix_sem.at[1, seq],
            device_id=(req, other),
            device_id_type=MESH,
        )
        got = pltpu.make_async_remote_copy(
            src_ref=mix_send.at[other],
            dst_ref=mix_recv.at[source],
            send_sem=mix_sem.at[0, k],
            recv_sem=mix_sem.at[1, source],
            device_id=(req, other),
            device_id_type=MESH,
        )
        return sent, got

    @pl.loop(1, n_seq)
    def _(k):
        other = lax.rem(seq + k, n_seq)
        mine = pl.ds(pl.multiple_of(other * mix_rows, 16), mix_rows)
        mix_send[other] = stage[:, mine, :].astype(jnp.bfloat16)
        mix_copy(k)[0].start()

    mix_recv[seq] = stage[:, pl.ds(pl.multiple_of(seq * mix_rows, 16), mix_rows), :].astype(
        jnp.bfloat16
    )

    sibling = (req, seq + 1 - 2 * core)
    their_output_rows = pl.ds(pl.multiple_of((1 - core) * 64, 64), 64)

    def pair_copies(to_rows, to_slot):
        return (
            pltpu.make_async_remote_copy(
                src_ref=output_hbm,
                dst_ref=output_buf.at[to_rows],
                send_sem=pair_sem.at[0],
                recv_sem=pair_sem.at[1],
                device_id=sibling,
                device_id_type=MESH,
            ),
            pltpu.make_async_remote_copy(
                src_ref=residual_buf.at[core],
                dst_ref=residual_buf.at[to_slot],
                send_sem=pair_sem.at[2],
                recv_sem=pair_sem.at[3],
                device_id=sibling,
                device_id_type=MESH,
            ),
        )

    pair_sends = pair_copies(my_output_rows, core)
    pair_gets = pair_copies(their_output_rows, 1 - core)
    for copy in pair_sends:
        copy.start()

    @pl.loop(1, n_seq)
    def _(k):
        mix_copy(k)[1].wait_recv()

    info = mix_recv[:, chunks].astype(jnp.float32)
    info_lane = lax.broadcasted_iota(jnp.int32, info.shape, 2)
    peaks = jnp.sum(jnp.where(info_lane < 3, info, 0.0), axis=2, keepdims=True)
    totals = jnp.sum(
        jnp.where(info_lane < 3, 0.0, info), axis=2, keepdims=True
    )
    rescale = jnp.exp(peaks - jnp.max(peaks, axis=0, keepdims=True))
    denominator = jnp.sum(rescale * totals, axis=0)
    local_copies[1].wait()
    attended = jnp.concatenate(
        [
            jnp.sum(rescale * mix_recv[:, c].astype(jnp.float32), axis=0) / denominator
            for c in range(chunks)
        ],
        axis=1,
    )
    upper_part = attended.astype(jnp.bfloat16)
    lower_part = (attended - upper_part.astype(jnp.float32)).astype(jnp.bfloat16)
    value_size = value_buf.shape[2]
    for j in range(own_heads):
        span = slice(j * rows, (j + 1) * rows)
        made = jnp.dot(upper_part[span], value_buf[j], preferred_element_type=jnp.float32)
        made += jnp.dot(lower_part[span], value_buf[j], preferred_element_type=jnp.float32)
        heads_send[:, j * value_size : (j + 1) * value_size] = made.astype(jnp.bfloat16)

    head_cols = own_heads * value_size
    wanted_core = lax.div(req, n_req // 2)
    in_half = n_req // 2

    def heads_slot(r, s):
        return heads_full.at[
            pl.ds(pl.multiple_of(lax.rem(r, in_half) * rows, rows), rows),
            pl.ds(pl.multiple_of(s * head_cols, 128), head_cols),
        ]

    def heads_copy(target, r, s):
        return pltpu.make_async_remote_copy(
            src_ref=heads_send,
            dst_ref=heads_slot(r, s),
            send_sem=heads_sem.at[0, lax.div(target, 2)],
            recv_sem=heads_sem.at[1, lax.rem(r, in_half) * n_seq + s],
            device_id=place(target),
            device_id_type=MESH,
        )

    @pl.loop(0, n_pair)
    def _(k):
        target = lax.rem(pair + 1 + k, n_pair) * 2 + wanted_core

        @pl.when(target != me)
        def _():
            heads_copy(target, req, seq).start()

    @pl.when(core == wanted_core)
    def _():
        heads_slot(req, seq)[...] = heads_send[...]

    for copy in pair_gets:
        copy.wait_recv()
    local_copies[2].wait()

    @pl.loop(0, n_pair)
    def _(k):
        r = core * in_half + lax.div(k, n_seq)
        s = lax.rem(k, n_seq)

        @pl.when(r * n_seq + s != me)
        def _():
            heads_copy(core, r, s).wait_recv()

    my_rows = pl.ds(pl.multiple_of(core * half, half), half)
    my_cols = pl.ds(pl.multiple_of(pair * 128, 128), 128)
    attn_out = lax.dot_general(
        heads_full[...], output_buf[...], NT, preferred_element_type=jnp.float32
    )
    entering = jnp.concatenate(
        [residual_buf[0, my_rows, :], residual_buf[1, my_rows, :]], axis=1
    ).astype(jnp.float32)
    stream_full[my_rows, my_cols] = (entering + attn_out).astype(jnp.bfloat16)

    their_rows = pl.ds(pl.multiple_of((1 - core) * half, half), half)

    def chip(p):
        return place(lax.rem(p, n_pair) * 2 + core)

    def spread_copy(ref, sem, k, owner):
        block = ref.at[my_rows, pl.ds(pl.multiple_of(owner * 128, 128), 128)]
        return pltpu.make_async_remote_copy(
            src_ref=block,
            dst_ref=block,
            send_sem=sem.at[0, k],
            recv_sem=sem.at[1, owner],
            device_id=chip(pair + k),
            device_id_type=MESH,
        )

    def half_copy(ref, sem, span):
        return pltpu.make_async_remote_copy(
            src_ref=ref.at[span],
            dst_ref=ref.at[span],
            send_sem=sem.at[0, 0],
            recv_sem=sem.at[1, n_pair],
            device_id=sibling,
            device_id_type=MESH,
        )

    def spread(ref, sem):
        @pl.loop(1, n_pair)
        def _(k):
            spread_copy(ref, sem, k, pair).start()

    def collect(ref, sem):
        @pl.loop(1, n_pair)
        def _(k):
            spread_copy(ref, sem, k, lax.rem(pair + n_pair - k, n_pair)).wait_recv()

        half_copy(ref, sem, my_rows).start()
        half_copy(ref, sem, their_rows).wait_recv()

    spread(stream_full, stream_sem)
    for copy in local_copies[3:]:
        copy.wait()
    collect(stream_full, stream_sem)
    normed_buf[...] = normed(stream_full[...], middle_gain_ref[...])

    def glu(gate_rows, up_rows):
        hidden = normed_buf[...]
        gate = lax.dot_general(hidden, gate_rows, NT, preferred_element_type=jnp.float32)
        upper = lax.dot_general(hidden, up_rows, NT, preferred_element_type=jnp.float32)
        return (gate / (1.0 + jnp.exp(-gate)) * upper).astype(jnp.bfloat16)

    spans = [slice(c * 512, (c + 1) * 512) for c in range(width // 512)]
    shared_act = glu(shared_gate_buf[...], shared_up_buf[...])
    for span in spans:
        moe_acc[:, span] = jnp.dot(
            shared_act, shared_down_buf[:, span], preferred_element_type=jnp.float32
        )

    @pl.loop(0, experts)
    def _(e):
        for which in range(3):
            expert_copy(which, e).wait()
        share = jnp.sum(
            jnp.where(routes_ref[...] == seq * experts + e, route_weights_ref[...], 0.0),
            axis=1,
            keepdims=True,
        )
        act = glu(gate_buf[e], up_buf[e])
        for span in spans:
            moe_acc[:, span] += share * jnp.dot(
                act, down_buf[e, :, span], preferred_element_type=jnp.float32
            )

    moe_send[...] = moe_acc[their_rows, :].astype(jnp.bfloat16)
    moe_half = pltpu.make_async_remote_copy(
        src_ref=moe_send,
        dst_ref=moe_theirs,
        send_sem=moe_sem.at[0, 0],
        recv_sem=moe_sem.at[1, n_pair],
        device_id=sibling,
        device_id_type=MESH,
    )
    moe_half.start()
    moe_half.wait_recv()
    moe_sums[...] = (moe_acc[my_rows, :] + moe_theirs[...].astype(jnp.float32)).astype(
        jnp.bfloat16
    )

    def moe_copy(k, owner):
        target = lax.rem(pair + k, n_pair)
        return pltpu.make_async_remote_copy(
            src_ref=moe_sums.at[:, pl.ds(pl.multiple_of(target * 128, 128), 128)],
            dst_ref=moe_recv.at[owner],
            send_sem=moe_sem.at[0, k],
            recv_sem=moe_sem.at[1, owner],
            device_id=chip(target),
            device_id_type=MESH,
        )

    @pl.loop(1, n_pair)
    def _(k):
        moe_copy(k, pair).start()

    moe_recv[pair] = moe_sums[:, my_cols]

    @pl.loop(1, n_pair)
    def _(k):
        moe_copy(k, lax.rem(pair + n_pair - k, n_pair)).wait_recv()

    moe = jnp.sum(moe_recv[...].astype(jnp.float32), axis=0)
    layer_full[my_rows, my_cols] = (
        stream_full[my_rows, my_cols].astype(jnp.float32) + moe
    ).astype(jnp.bfloat16)
    spread(layer_full, layer_sem)
    collect(layer_full, layer_sem)
    shown = layer_full[:, my_cols].astype(jnp.float32)
    layer_ref[...] = jnp.where(core == 0, shown[:, :64], shown[:, 64:]).astype(jnp.bfloat16)
    normed_buf[...] = normed(layer_full[...], final_gain_ref[...])

    lowest = jnp.full((tokens, 128), -jnp.inf, jnp.float32)

    def vocab_step(v, state):
        first, second = state
        unembed_copy(v).wait()
        logits = lax.dot_general(
            normed_buf[...],
            unembed_buf[pl.ds(pl.multiple_of(v * piece, 64), piece), :],
            NT,
            preferred_element_type=jnp.float32,
        )
        for c in range(piece // 128):
            part = logits[:, c * 128 : (c + 1) * 128]
            second = jnp.maximum(second, jnp.minimum(first, part))
            first = jnp.maximum(first, part)
        return first, second

    first, second = lax.fori_loop(0, VOCAB_PIECES, vocab_step, (lowest, lowest))
    token_lane = lax.broadcasted_iota(jnp.int32, (tokens, 128), 1)
    top = jnp.max(first, axis=1, keepdims=True)
    where_top = jnp.min(
        jnp.where(first == top, token_lane, 128), axis=1, keepdims=True
    )
    runner = jnp.max(
        jnp.where(token_lane == where_top, second, first), axis=1, keepdims=True
    )
    packed = jnp.where(token_lane == 0, top, runner)
    packed = jnp.concatenate([packed, packed], axis=0).T
    best_send[...] = packed[:8]
    best_half = pltpu.make_async_remote_copy(
        src_ref=best_send,
        dst_ref=best_theirs,
        send_sem=best_sem.at[0, 0],
        recv_sem=best_sem.at[1, n_pair],
        device_id=sibling,
        device_id_type=MESH,
    )
    best_half.start()
    best_half.wait_recv()

    def joined(a, b):
        return (
            jnp.maximum(a[0], b[0]),
            jnp.maximum(jnp.minimum(a[0], b[0]), jnp.maximum(a[1], b[1])),
        )

    chip_best = joined(
        (best_send[0:1, :], best_send[1:2, :]), (best_theirs[0:1, :], best_theirs[1:2, :])
    )
    best_sums[0:1, :] = chip_best[0]
    best_sums[1:8, :] = jnp.broadcast_to(chip_best[1], (7, 128))
    best_recv[pair] = best_sums[...]

    def best_copy(k, owner):
        return pltpu.make_async_remote_copy(
            src_ref=best_sums,
            dst_ref=best_recv.at[owner],
            send_sem=best_sem.at[0, k],
            recv_sem=best_sem.at[1, owner],
            device_id=chip(pair + k),
            device_id_type=MESH,
        )

    @pl.loop(1, n_pair)
    def _(k):
        best_copy(k, pair).start()

    moe_half.wait_send()
    best_half.wait_send()
    half_copy(stream_full, stream_sem, my_rows).wait_send()
    half_copy(layer_full, layer_sem, my_rows).wait_send()

    for copy in pair_sends:
        copy.wait_send()

    @pl.loop(1, n_seq)
    def _(k):
        mix_copy(k)[0].wait_send()

    @pl.loop(0, n_pair)
    def _(k):
        target = k * 2 + wanted_core

        @pl.when(target != me)
        def _():
            heads_copy(target, req, seq).wait_send()

    @pl.loop(1, n_pair)
    def _(k):
        spread_copy(stream_full, stream_sem, k, pair).wait_send()
        moe_copy(k, pair).wait_send()
        spread_copy(layer_full, layer_sem, k, pair).wait_send()

    @pl.loop(1, n_pair)
    def _(k):
        best_copy(k, lax.rem(pair + n_pair - k, n_pair)).wait_recv()

    found = [best_recv[d] for d in range(n_pair)]
    pairs = [(x[0:1], x[1:2]) for x in found]
    while len(pairs) > 1:
        pairs = [joined(a, b) for a, b in zip(pairs[0::2], pairs[1::2])]
    best_ref[0:1, :] = pairs[0][0][:, :tokens]
    best_ref[1:2, :] = pairs[0][1][:, :tokens]

    @pl.loop(1, n_pair)
    def _(k):
        best_copy(k, pair).wait_send()


def fits(n_req, n_seq, shapes):
    residual, query, cache, unembed = shapes
    return (
        n_req % 2 == 0
        and n_seq % 2 == 0
        and query[1] % n_seq == 0
        and query[0] % 16 == 0
        and residual[1] == 64
        and residual[0] == 64
        and cache[1] % 128 == 0
        and unembed[0] % (128 * VOCAB_PIECES) == 0
        and n_req * n_seq & (n_req * n_seq - 1) == 0
    )


def fused(
    n_req,
    n_seq,
    residual,
    query_plain,
    query_rotary,
    latent_cache,
    rotary_cache,
    lengths,
    absorb_key,
    absorb_value,
    output_weight,
    middle_gain,
    routes,
    route_weights,
    gate_weight,
    up_weight,
    down_weight,
    shared_gate,
    shared_up,
    shared_down,
    final_gain,
    unembed,
):
    query_latent = jnp.einsum(
        "rhn,hnc->rhc", query_plain, absorb_key, preferred_element_type=jnp.float32
    ).astype(jnp.bfloat16)
    rows, heads, latent = query_latent.shape
    tokens = residual.shape[0]
    width = unembed.shape[1]
    n_dev = n_req * n_seq
    block_len = latent_cache.shape[1]
    experts, ff = gate_weight.shape[0], gate_weight.shape[2]
    shared_ff = shared_gate.shape[1]
    own_heads = heads // n_seq
    value_size = absorb_value.shape[2]
    parts = latent // 128 + 1
    bf, f32 = jnp.bfloat16, jnp.float32
    dma = pltpu.SemaphoreType.DMA
    vmem = pl.BlockSpec(memory_space=pltpu.VMEM)
    anywhere = pl.BlockSpec(memory_space=pl.ANY)
    layer_out, best = pl.pallas_call(
        functools.partial(layer_kernel, n_req, n_seq, query_plain.shape[2]),
        name="layer",
        out_shape=(
            jax.ShapeDtypeStruct(residual.shape, bf),
            jax.ShapeDtypeStruct((2, tokens), f32),
        ),
        in_specs=[pl.BlockSpec(memory_space=pltpu.SMEM)] + [vmem] * 7 + [anywhere] * 11,
        out_specs=(vmem, vmem),
        scratch_shapes=[
            pltpu.VMEM((SLOTS, block_len, latent), bf),
            pltpu.VMEM(rotary_cache.shape, bf),
            pltpu.VMEM((own_heads, latent, value_size), bf),
            pltpu.VMEM((128, width), bf),
            pltpu.VMEM((2, tokens, 64), bf),
            pltpu.VMEM((experts, ff, width), bf),
            pltpu.VMEM((experts, ff, width), bf),
            pltpu.VMEM((experts, ff, width), bf),
            pltpu.VMEM((shared_ff, width), bf),
            pltpu.VMEM((shared_ff, width), bf),
            pltpu.VMEM((shared_ff, width), bf),
            pltpu.VMEM(unembed.shape, bf),
            pltpu.VMEM((parts, heads * rows, 128), f32),
            pltpu.VMEM((n_seq, parts, own_heads * rows, 128), bf),
            pltpu.VMEM((n_seq, parts, own_heads * rows, 128), bf),
            pltpu.VMEM((rows, own_heads * value_size), bf),
            pltpu.VMEM((tokens // 2, heads * value_size), bf),
            pltpu.VMEM((tokens, width), bf),
            pltpu.VMEM((tokens, width), bf),
            pltpu.VMEM((tokens, width), f32),
            pltpu.VMEM((tokens // 2, width), bf),
            pltpu.VMEM((tokens // 2, width), bf),
            pltpu.VMEM((tokens // 2, width), bf),
            pltpu.VMEM((n_dev // 2, tokens // 2, 128), bf),
            pltpu.VMEM((tokens, width), bf),
            pltpu.VMEM((8, 128), f32),
            pltpu.VMEM((8, 128), f32),
            pltpu.VMEM((8, 128), f32),
            pltpu.VMEM((n_dev // 2, 8, 128), f32),
            dma((SLOTS,)),
            dma((6,)),
            dma((3, experts)),
            dma((VOCAB_PIECES,)),
            dma((4,)),
            dma((2, n_seq)),
            dma((2, n_dev // 2)),
            dma((2, n_dev // 2 + 1)),
            dma((2, n_dev // 2 + 1)),
            dma((2, n_dev // 2 + 1)),
            dma((2, n_dev // 2 + 1)),
        ],
        compiler_params=pltpu.CompilerParams(
            collective_id=0, has_side_effects=True, vmem_limit_bytes=63 * 1024 * 1024
        ),
    )(
        lengths,
        query_latent,
        query_rotary,
        residual,
        routes,
        route_weights,
        middle_gain.reshape(1, width),
        final_gain.reshape(1, width),
        latent_cache,
        rotary_cache,
        absorb_value,
        output_weight.T,
        jnp.swapaxes(gate_weight, 1, 2),
        jnp.swapaxes(up_weight, 1, 2),
        down_weight,
        shared_gate.T,
        shared_up.T,
        shared_down,
        unembed,
    )
    return layer_out, best.T


def chosen(n_req, n_seq, *args):
    shapes = (args[0].shape, args[1].shape, args[3].shape, args[19].shape)
    if fits(n_req, n_seq, shapes):
        return fused(n_req, n_seq, *args)
    return local(*args)


def solution(mesh):
    in_specs = (
        P(None, ("req", "seq")),
        P("req", None, None),
        P("req", None, None),
        P("req", "seq", None),
        P("req", None, "seq"),
        P("req"),
        P(),
        P(),
        P(None, ("req", "seq")),
        P(),
        P(),
        P(),
        P("seq", None, "req"),
        P("seq", None, "req"),
        P("seq", "req", None),
        P(None, ("req", "seq")),
        P(None, ("req", "seq")),
        P(("req", "seq"), None),
        P(),
        P(("req", "seq"), None),
    )
    out_specs = (P(None, ("req", "seq")), P())
    body = functools.partial(chosen, mesh.shape["req"], mesh.shape["seq"])
    return jax.shard_map(body, mesh=mesh, in_specs=in_specs, out_specs=out_specs, check_vma=False)
```

```python
import functools
import jax
import jax.numpy as jnp
from jax import lax
from jax.experimental import pallas as pl
from jax.experimental.pallas import tpu as pltpu
from jax.sharding import PartitionSpec as P

NEG_FILL = -1e30
NORM_EPS = 1e-06


def combined_all(x, axis, join):
    gathered = jax.tree.map(
        lambda a, kind: lax.all_gather(a.astype(kind), axis),
        x,
        (jnp.bfloat16, jnp.bfloat16, jnp.bfloat16),
    )

    def take(source):
        return jax.tree.map(
            lambda a, own: lax.dynamic_index_in_dim(a, source, 0, False).astype(own.dtype),
            gathered,
            x,
        )

    return lax.fori_loop(
        1, lax.axis_size(axis), lambda source, state: join(state, take(source)), take(0)
    )


def merged_2(x, axis, combine):
    everything = lax.all_gather(x, axis)
    first = everything[0]

    def hop(k, so_far):
        return combine(so_far, everything[k])

    return lax.fori_loop(1, lax.axis_size(axis), hop, first)


def normed(hidden, gain):
    widened = hidden.astype(jnp.float32)
    meansq = jnp.mean(widened * widened, axis=-1, keepdims=True)
    return (widened * lax.rsqrt(meansq + NORM_EPS) * gain).astype(jnp.bfloat16)


def blend(former, latter):
    largest = jnp.maximum(former[0], latter[0])
    former_rescale = jnp.exp(former[0] - largest)
    latter_rescale = jnp.exp(latter[0] - largest)
    totals = former_rescale * former[1] + latter_rescale * latter[1]
    mixes = former_rescale[..., None] * former[2] + latter_rescale[..., None] * latter[2]
    return (largest, totals, mixes)


def best_two(former, latter):
    higher = jnp.maximum(former[:, 0], latter[:, 0])
    lower = jnp.maximum(
        jnp.minimum(former[:, 0], latter[:, 0]), jnp.maximum(former[:, 1], latter[:, 1])
    )
    return jnp.stack([higher, lower], axis=1)


def local(
    residual,
    query_plain,
    query_rotary,
    latent_cache,
    rotary_cache,
    lengths,
    absorb_key,
    absorb_value,
    output_weight,
    middle_gain,
    routes,
    route_weights,
    gate_weight,
    up_weight,
    down_weight,
    shared_gate,
    shared_up,
    shared_down,
    final_gain,
    unembed,
):
    group_rows, head_count, plain_size = query_plain.shape
    block_len = latent_cache.shape[1]
    value_size = absorb_value.shape[2]
    score_scale = (plain_size + query_rotary.shape[2]) ** (-0.5)
    value_wide = absorb_value.astype(jnp.float32)
    query_latent = jnp.einsum(
        "rhn,hnc->rhc", query_plain, absorb_key, preferred_element_type=jnp.float32
    ).astype(jnp.bfloat16)
    scores = jnp.einsum(
        "rhc,rtc->rht", query_latent, latent_cache, preferred_element_type=jnp.float32
    )
    scores = (
        scores
        + jnp.einsum("rhj,rjt->rht", query_rotary, rotary_cache, preferred_element_type=jnp.float32)
    ) * score_scale
    position = lax.axis_index("seq") * block_len + lax.broadcasted_iota(
        jnp.int32, (1, 1, block_len), 2
    )
    usable = position < lengths[:, None, None]
    block_peak = jnp.max(jnp.where(usable, scores, NEG_FILL), axis=2)
    weights = jnp.where(usable, jnp.exp(scores - block_peak[:, :, None]), 0.0).astype(jnp.bfloat16)
    block_total = jnp.sum(weights.astype(jnp.float32), axis=2)
    block_mix = jnp.einsum(
        "rht,rtc->rhc", weights, latent_cache, preferred_element_type=jnp.float32
    )
    merged_peak, merged_total, merged_mix = combined_all(
        (block_peak, block_total, block_mix), "seq", blend
    )
    merged = merged_mix / merged_total[:, :, None]
    merged = jnp.einsum("rhc,hcv->rhv", merged, value_wide, precision=lax.Precision.HIGHEST)
    group_output = merged.astype(jnp.bfloat16).reshape(group_rows, head_count * value_size)
    attn_out = jnp.dot(
        lax.all_gather(group_output, "req", axis=0, tiled=True),
        output_weight,
        preferred_element_type=jnp.float32,
    )
    column_count = residual.shape[1]
    stream_cols = (residual.astype(jnp.float32) + attn_out).astype(jnp.bfloat16)
    stream = lax.all_gather(stream_cols, ("req", "seq"), axis=1, tiled=True)
    expert_in = normed(stream, middle_gain)
    local_count = gate_weight.shape[0]
    expert_index = lax.axis_index("seq") * local_count + lax.broadcasted_iota(
        jnp.int32, (local_count, 1, 1), 0
    )
    route_share = jnp.sum(
        jnp.where(routes[None, :, :] == expert_index, route_weights[None, :, :], 0.0), axis=2
    )
    gate = jnp.einsum("td,edf->etf", expert_in, gate_weight, preferred_element_type=jnp.float32)
    upper = jnp.einsum("td,edf->etf", expert_in, up_weight, preferred_element_type=jnp.float32)
    expert_act = (jax.nn.silu(gate) * upper).astype(jnp.bfloat16)
    expert_back = jnp.einsum(
        "etf,efd->etd", expert_act, down_weight, preferred_element_type=jnp.float32
    )
    shared_gated = jnp.dot(expert_in, shared_gate, preferred_element_type=jnp.float32)
    shared_upper = jnp.dot(expert_in, shared_up, preferred_element_type=jnp.float32)
    shared_act = (jax.nn.silu(shared_gated) * shared_upper).astype(jnp.bfloat16)
    shared_back = jnp.dot(shared_act, shared_down, preferred_element_type=jnp.float32)
    expert_term = jnp.sum(route_share[:, :, None] * expert_back, axis=0) + shared_back
    column_start = lax.axis_index(("req", "seq")) * column_count
    moe = lax.psum(expert_term, ("req", "seq"))
    layer_full = (stream.astype(jnp.float32) + moe).astype(jnp.bfloat16)
    layer_out = lax.dynamic_slice_in_dim(layer_full, column_start, column_count, 1)
    final_in = normed(layer_full, final_gain)
    logits = lax.dot_general(
        final_in, unembed, (((1,), (1,)), ((), ())), preferred_element_type=jnp.float32
    )
    local_best = lax.top_k(logits, 2)[0]
    best_logits = merged_2(local_best, ("req", "seq"), best_two)
    return (layer_out, best_logits)


NT = (((1,), (1,)), ((), ()))
VOCAB_PIECES = 5
MESH = pl.DeviceIdType.MESH


def layer_kernel(
    n_req,
    n_seq,
    lengths_ref,
    query_plain_ref,
    query_rotary_ref,
    residual_ref,
    routes_ref,
    route_weights_ref,
    middle_gain_ref,
    final_gain_ref,
    latent_hbm,
    rotary_hbm,
    key_hbm,
    value_hbm,
    output_hbm,
    gate_hbm,
    up_hbm,
    down_hbm,
    shared_gate_hbm,
    shared_up_hbm,
    shared_down_hbm,
    unembed_hbm,
    layer_ref,
    best_ref,
    latent_buf,
    rotary_buf,
    key_buf,
    query_wide,
    query_latent,
    value_buf,
    output_buf,
    residual_buf,
    gate_buf,
    up_buf,
    down_buf,
    shared_gate_buf,
    shared_up_buf,
    shared_down_buf,
    unembed_buf,
    stage,
    mix_send,
    mix_recv,
    heads_send,
    heads_full,
    stream_full,
    normed_buf,
    share_buf,
    moe_acc,
    moe_send,
    moe_theirs,
    moe_sums,
    moe_recv,
    layer_full,
    best_send,
    best_theirs,
    best_sums,
    best_recv,
    latent_sem,
    local_sem,
    expert_sem,
    unembed_sem,
    pair_sem,
    mix_sem,
    heads_sem,
    stream_sem,
    moe_sem,
    layer_sem,
    best_sem,
):
    n_dev = n_req * n_seq
    n_pair = n_dev // 2
    rows, heads, plain_size = query_plain_ref.shape
    latent = latent_hbm.shape[2]
    block_len = latent_hbm.shape[1]
    experts = gate_hbm.shape[0]
    tokens, width = stream_full.shape
    half = tokens // 2
    own_heads = heads // n_seq
    mix_rows = own_heads * rows
    chunks = latent // 128
    score_scale = (plain_size + query_rotary_ref.shape[2]) ** (-0.5)
    req = lax.axis_index("req")
    seq = lax.axis_index("seq")
    me = req * n_seq + seq
    core = lax.rem(seq, 2)
    pair = lax.div(me, 2)

    def place(d):
        return (lax.div(d, n_seq), lax.rem(d, n_seq))

    barrier = pltpu.get_barrier_semaphore()

    @pl.loop(1, n_dev)
    def _(k):
        pl.semaphore_signal(
            barrier, inc=1, device_id=place(lax.rem(me + k, n_dev)), device_id_type=MESH
        )

    def latent_copy(i):
        return pltpu.make_async_copy(latent_hbm.at[i], latent_buf.at[i], latent_sem.at[i])

    my_output_rows = pl.ds(pl.multiple_of(core * 64, 64), 64)
    local_copies = [
        pltpu.make_async_copy(rotary_hbm, rotary_buf, local_sem.at[0]),
        pltpu.make_async_copy(
            value_hbm.at[pl.ds(seq * own_heads, own_heads)], value_buf, local_sem.at[1]
        ),
        pltpu.make_async_copy(output_hbm, output_buf.at[my_output_rows], local_sem.at[2]),
        pltpu.make_async_copy(shared_gate_hbm, shared_gate_buf, local_sem.at[3]),
        pltpu.make_async_copy(shared_up_hbm, shared_up_buf, local_sem.at[4]),
        pltpu.make_async_copy(shared_down_hbm, shared_down_buf, local_sem.at[5]),
    ]

    key_copy = pltpu.make_async_copy(key_hbm, key_buf, local_sem.at[6])

    def expert_copy(which, e):
        source, target = ((gate_hbm, gate_buf), (up_hbm, up_buf), (down_hbm, down_buf))[which]
        return pltpu.make_async_copy(source.at[e], target.at[e], expert_sem.at[which, e])

    piece = unembed_hbm.shape[0] // VOCAB_PIECES

    def unembed_copy(v):
        place_rows = pl.ds(pl.multiple_of(v * piece, 64), piece)
        return pltpu.make_async_copy(
            unembed_hbm.at[place_rows], unembed_buf.at[place_rows], unembed_sem.at[v]
        )

    key_copy.start()
    local_copies[0].start()

    @pl.loop(0, rows)
    def _(i):
        latent_copy(i).start()

    for copy in local_copies[1:]:
        copy.start()
    residual_buf[core] = residual_ref[...]
    for r in range(rows):
        query_wide[r * heads : (r + 1) * heads, :] = query_plain_ref[r].astype(jnp.float32)
    key_copy.wait()
    for h in range(heads):
        made = jnp.dot(
            query_wide[pl.ds(h, rows, stride=heads), :].astype(jnp.bfloat16),
            key_buf[h],
            preferred_element_type=jnp.float32,
        )
        for c in range(chunks):
            query_latent[c, pl.ds(h, rows, stride=heads), :] = made[:, c * 128 : (c + 1) * 128]
    local_copies[0].wait()

    lane = lax.broadcasted_iota(jnp.int32, (heads, 128), 1)
    position = seq * block_len + lax.broadcasted_iota(jnp.int32, (heads, block_len), 1)

    @pl.loop(0, rows)
    def _(i):
        latent_copy(i).wait()
        cached = latent_buf[i]
        here = pl.ds(pl.multiple_of(i * heads, heads), heads)
        query = jnp.concatenate([query_latent[c, here, :] for c in range(chunks)], axis=1)
        scores = lax.dot_general(
            query.astype(jnp.bfloat16), cached, NT, preferred_element_type=jnp.float32
        )
        scores = (
            scores
            + jnp.dot(query_rotary_ref[i], rotary_buf[i], preferred_element_type=jnp.float32)
        ) * score_scale
        usable = position < lengths_ref[i]
        peak = jnp.max(jnp.where(usable, scores, NEG_FILL), axis=1, keepdims=True)
        weights = jnp.where(usable, jnp.exp(scores - peak), 0.0).astype(jnp.bfloat16)
        total = jnp.sum(weights.astype(jnp.float32), axis=1, keepdims=True)
        mix = jnp.dot(weights, cached, preferred_element_type=jnp.float32)
        for c in range(chunks):
            stage[c, pl.ds(i, heads, stride=rows), :] = mix[:, c * 128 : (c + 1) * 128]
        info = jnp.zeros((heads, 128), jnp.float32)
        at = 0
        for value in (peak, total):
            rest = value
            for _ in range(3):
                part = rest.astype(jnp.bfloat16).astype(jnp.float32)
                info = jnp.where(lane == at, part, info)
                rest = rest - part
                at += 1
        stage[chunks, pl.ds(i, heads, stride=rows), :] = info

        @pl.when(i < experts)
        def _():
            expert_copy(0, i).start()
            expert_copy(1, i).start()
            expert_copy(2, i).start()

    for v in range(VOCAB_PIECES):
        unembed_copy(v).start()

    pl.semaphore_wait(barrier, n_dev - 1)

    def mix_copy(k):
        other = lax.rem(seq + k, n_seq)
        source = lax.rem(seq + n_seq - k, n_seq)
        sent = pltpu.make_async_remote_copy(
            src_ref=mix_send.at[other],
            dst_ref=mix_recv.at[seq],
            send_sem=mix_sem.at[0, k],
            recv_sem=mix_sem.at[1, seq],
            device_id=(req, other),
            device_id_type=MESH,
        )
        got = pltpu.make_async_remote_copy(
            src_ref=mix_send.at[other],
            dst_ref=mix_recv.at[source],
            send_sem=mix_sem.at[0, k],
            recv_sem=mix_sem.at[1, source],
            device_id=(req, other),
            device_id_type=MESH,
        )
        return sent, got

    @pl.loop(1, n_seq)
    def _(k):
        other = lax.rem(seq + k, n_seq)
        mine = pl.ds(pl.multiple_of(other * mix_rows, 16), mix_rows)
        mix_send[other] = stage[:, mine, :].astype(jnp.bfloat16)
        mix_copy(k)[0].start()

    mix_recv[seq] = stage[:, pl.ds(pl.multiple_of(seq * mix_rows, 16), mix_rows), :].astype(
        jnp.bfloat16
    )

    sibling = (req, seq + 1 - 2 * core)
    their_output_rows = pl.ds(pl.multiple_of((1 - core) * 64, 64), 64)

    def pair_copies(to_rows, to_slot):
        return (
            pltpu.make_async_remote_copy(
                src_ref=output_hbm,
                dst_ref=output_buf.at[to_rows],
                send_sem=pair_sem.at[0],
                recv_sem=pair_sem.at[1],
                device_id=sibling,
                device_id_type=MESH,
            ),
            pltpu.make_async_remote_copy(
                src_ref=residual_buf.at[core],
                dst_ref=residual_buf.at[to_slot],
                send_sem=pair_sem.at[2],
                recv_sem=pair_sem.at[3],
                device_id=sibling,
                device_id_type=MESH,
            ),
        )

    pair_sends = pair_copies(my_output_rows, core)
    pair_gets = pair_copies(their_output_rows, 1 - core)
    for copy in pair_sends:
        copy.start()

    for e in range(experts):
        share_row = jnp.sum(
            jnp.where(routes_ref[...] == seq * experts + e, route_weights_ref[...], 0.0),
            axis=0,
            keepdims=True,
        )
        share_buf[e] = jnp.broadcast_to(share_row, (128, tokens)).T

    @pl.loop(1, n_seq)
    def _(k):
        mix_copy(k)[1].wait_recv()

    info = mix_recv[:, chunks].astype(jnp.float32)
    info_lane = lax.broadcasted_iota(jnp.int32, info.shape, 2)
    peaks = jnp.sum(jnp.where(info_lane < 3, info, 0.0), axis=2, keepdims=True)
    totals = jnp.sum(
        jnp.where(info_lane < 3, 0.0, info), axis=2, keepdims=True
    )
    rescale = jnp.exp(peaks - jnp.max(peaks, axis=0, keepdims=True))
    denominator = jnp.sum(rescale * totals, axis=0)
    local_copies[1].wait()
    attended = jnp.concatenate(
        [
            jnp.sum(rescale * mix_recv[:, c].astype(jnp.float32), axis=0) / denominator
            for c in range(chunks)
        ],
        axis=1,
    )
    upper_part = attended.astype(jnp.bfloat16)
    lower_part = (attended - upper_part.astype(jnp.float32)).astype(jnp.bfloat16)
    value_size = value_buf.shape[2]
    for j in range(own_heads):
        span = slice(j * rows, (j + 1) * rows)
        made = jnp.dot(upper_part[span], value_buf[j], preferred_element_type=jnp.float32)
        made += jnp.dot(lower_part[span], value_buf[j], preferred_element_type=jnp.float32)
        heads_send[:, j * value_size : (j + 1) * value_size] = made.astype(jnp.bfloat16)

    head_cols = own_heads * value_size
    wanted_core = lax.div(req, n_req // 2)
    in_half = n_req // 2

    def heads_slot(r, s):
        return heads_full.at[
            pl.ds(pl.multiple_of(lax.rem(r, in_half) * rows, rows), rows),
            pl.ds(pl.multiple_of(s * head_cols, 128), head_cols),
        ]

    def heads_copy(target, r, s):
        return pltpu.make_async_remote_copy(
            src_ref=heads_send,
            dst_ref=heads_slot(r, s),
            send_sem=heads_sem.at[0, lax.div(target, 2)],
            recv_sem=heads_sem.at[1, lax.rem(r, in_half) * n_seq + s],
            device_id=place(target),
            device_id_type=MESH,
        )

    @pl.loop(0, n_pair)
    def _(k):
        target = lax.rem(pair + 1 + k, n_pair) * 2 + wanted_core

        @pl.when(target != me)
        def _():
            heads_copy(target, req, seq).start()

    @pl.when(core == wanted_core)
    def _():
        heads_slot(req, seq)[...] = heads_send[...]

    for copy in pair_gets:
        copy.wait_recv()
    local_copies[2].wait()

    @pl.loop(0, n_pair)
    def _(k):
        r = core * in_half + lax.div(k, n_seq)
        s = lax.rem(k, n_seq)

        @pl.when(r * n_seq + s != me)
        def _():
            heads_copy(core, r, s).wait_recv()

    my_rows = pl.ds(pl.multiple_of(core * half, half), half)
    my_cols = pl.ds(pl.multiple_of(pair * 128, 128), 128)
    attn_out = lax.dot_general(
        heads_full[...], output_buf[...], NT, preferred_element_type=jnp.float32
    )
    entering = jnp.concatenate(
        [residual_buf[0, my_rows, :], residual_buf[1, my_rows, :]], axis=1
    ).astype(jnp.float32)
    stream_full[my_rows, my_cols] = (entering + attn_out).astype(jnp.bfloat16)

    their_rows = pl.ds(pl.multiple_of((1 - core) * half, half), half)

    def chip(p):
        return place(lax.rem(p, n_pair) * 2 + core)

    def spread_copy(ref, sem, k, owner):
        block = ref.at[my_rows, pl.ds(pl.multiple_of(owner * 128, 128), 128)]
        return pltpu.make_async_remote_copy(
            src_ref=block,
            dst_ref=block,
            send_sem=sem.at[0, k],
            recv_sem=sem.at[1, owner],
            device_id=chip(pair + k),
            device_id_type=MESH,
        )

    def half_copy(ref, sem, span):
        return pltpu.make_async_remote_copy(
            src_ref=ref.at[span],
            dst_ref=ref.at[span],
            send_sem=sem.at[0, 0],
            recv_sem=sem.at[1, n_pair],
            device_id=sibling,
            device_id_type=MESH,
        )

    def spread(ref, sem):
        @pl.loop(1, n_pair)
        def _(k):
            spread_copy(ref, sem, k, pair).start()

    def collect(ref, sem):
        @pl.loop(1, n_pair)
        def _(k):
            spread_copy(ref, sem, k, lax.rem(pair + n_pair - k, n_pair)).wait_recv()

        half_copy(ref, sem, my_rows).start()
        half_copy(ref, sem, their_rows).wait_recv()

    spread(stream_full, stream_sem)
    for copy in local_copies[3:]:
        copy.wait()
    collect(stream_full, stream_sem)
    normed_buf[...] = normed(stream_full[...], middle_gain_ref[...])

    def glu(gate_rows, up_rows):
        hidden = normed_buf[...]
        gate = lax.dot_general(hidden, gate_rows, NT, preferred_element_type=jnp.float32)
        upper = lax.dot_general(hidden, up_rows, NT, preferred_element_type=jnp.float32)
        return (gate / (1.0 + jnp.exp(-gate)) * upper).astype(jnp.bfloat16)

    spans = [slice(c * 512, (c + 1) * 512) for c in range(width // 512)]
    shared_act = glu(shared_gate_buf[...], shared_up_buf[...])
    for span in spans:
        moe_acc[:, span] = jnp.dot(
            shared_act, shared_down_buf[:, span], preferred_element_type=jnp.float32
        )

    @pl.loop(0, experts)
    def _(e):
        for which in range(3):
            expert_copy(which, e).wait()
        share = jnp.concatenate([share_buf[e]] * 4, axis=1)
        act = glu(gate_buf[e], up_buf[e])
        for span in spans:
            moe_acc[:, span] += share * jnp.dot(
                act, down_buf[e, :, span], preferred_element_type=jnp.float32
            )

    moe_send[...] = moe_acc[their_rows, :].astype(jnp.bfloat16)
    moe_half = pltpu.make_async_remote_copy(
        src_ref=moe_send,
        dst_ref=moe_theirs,
        send_sem=moe_sem.at[0, 0],
        recv_sem=moe_sem.at[1, n_pair],
        device_id=sibling,
        device_id_type=MESH,
    )
    moe_half.start()
    moe_half.wait_recv()
    moe_sums[...] = (moe_acc[my_rows, :] + moe_theirs[...].astype(jnp.float32)).astype(
        jnp.bfloat16
    )

    def moe_copy(k, owner):
        target = lax.rem(pair + k, n_pair)
        return pltpu.make_async_remote_copy(
            src_ref=moe_sums.at[:, pl.ds(pl.multiple_of(target * 128, 128), 128)],
            dst_ref=moe_recv.at[owner],
            send_sem=moe_sem.at[0, k],
            recv_sem=moe_sem.at[1, owner],
            device_id=chip(target),
            device_id_type=MESH,
        )

    @pl.loop(1, n_pair)
    def _(k):
        moe_copy(k, pair).start()

    moe_recv[pair] = moe_sums[:, my_cols]

    @pl.loop(1, n_pair)
    def _(k):
        moe_copy(k, lax.rem(pair + n_pair - k, n_pair)).wait_recv()

    moe = jnp.sum(moe_recv[...].astype(jnp.float32), axis=0)
    layer_full[my_rows, my_cols] = (
        stream_full[my_rows, my_cols].astype(jnp.float32) + moe
    ).astype(jnp.bfloat16)
    spread(layer_full, layer_sem)
    collect(layer_full, layer_sem)
    shown = layer_full[:, my_cols].astype(jnp.float32)
    layer_ref[...] = jnp.where(core == 0, shown[:, :64], shown[:, 64:]).astype(jnp.bfloat16)
    normed_buf[...] = normed(layer_full[...], final_gain_ref[...])

    lowest = jnp.full((tokens, 128), -jnp.inf, jnp.float32)

    def vocab_step(v, state):
        first, second = state
        unembed_copy(v).wait()
        logits = lax.dot_general(
            normed_buf[...],
            unembed_buf[pl.ds(pl.multiple_of(v * piece, 64), piece), :],
            NT,
            preferred_element_type=jnp.float32,
        )
        for c in range(piece // 128):
            part = logits[:, c * 128 : (c + 1) * 128]
            second = jnp.maximum(second, jnp.minimum(first, part))
            first = jnp.maximum(first, part)
        return first, second

    first, second = lax.fori_loop(0, VOCAB_PIECES, vocab_step, (lowest, lowest))
    token_lane = lax.broadcasted_iota(jnp.int32, (tokens, 128), 1)
    top = jnp.max(first, axis=1, keepdims=True)
    where_top = jnp.min(
        jnp.where(first == top, token_lane, 128), axis=1, keepdims=True
    )
    runner = jnp.max(
        jnp.where(token_lane == where_top, second, first), axis=1, keepdims=True
    )
    packed = jnp.where(token_lane == 0, top, runner)
    packed = jnp.concatenate([packed, packed], axis=0).T
    best_send[...] = packed[:8]
    best_half = pltpu.make_async_remote_copy(
        src_ref=best_send,
        dst_ref=best_theirs,
        send_sem=best_sem.at[0, 0],
        recv_sem=best_sem.at[1, n_pair],
        device_id=sibling,
        device_id_type=MESH,
    )
    best_half.start()
    best_half.wait_recv()

    def joined(a, b):
        return (
            jnp.maximum(a[0], b[0]),
            jnp.maximum(jnp.minimum(a[0], b[0]), jnp.maximum(a[1], b[1])),
        )

    chip_best = joined(
        (best_send[0:1, :], best_send[1:2, :]), (best_theirs[0:1, :], best_theirs[1:2, :])
    )
    best_sums[0:1, :] = chip_best[0]
    best_sums[1:8, :] = jnp.broadcast_to(chip_best[1], (7, 128))
    best_recv[pair] = best_sums[...]

    def best_copy(k, owner):
        return pltpu.make_async_remote_copy(
            src_ref=best_sums,
            dst_ref=best_recv.at[owner],
            send_sem=best_sem.at[0, k],
            recv_sem=best_sem.at[1, owner],
            device_id=chip(pair + k),
            device_id_type=MESH,
        )

    @pl.loop(1, n_pair)
    def _(k):
        best_copy(k, pair).start()

    moe_half.wait_send()
    best_half.wait_send()
    half_copy(stream_full, stream_sem, my_rows).wait_send()
    half_copy(layer_full, layer_sem, my_rows).wait_send()

    for copy in pair_sends:
        copy.wait_send()

    @pl.loop(1, n_seq)
    def _(k):
        mix_copy(k)[0].wait_send()

    @pl.loop(0, n_pair)
    def _(k):
        target = k * 2 + wanted_core

        @pl.when(target != me)
        def _():
            heads_copy(target, req, seq).wait_send()

    @pl.loop(1, n_pair)
    def _(k):
        spread_copy(stream_full, stream_sem, k, pair).wait_send()
        moe_copy(k, pair).wait_send()
        spread_copy(layer_full, layer_sem, k, pair).wait_send()

    @pl.loop(1, n_pair)
    def _(k):
        best_copy(k, lax.rem(pair + n_pair - k, n_pair)).wait_recv()

    found = [best_recv[d] for d in range(n_pair)]
    pairs = [(x[0:1], x[1:2]) for x in found]
    while len(pairs) > 1:
        pairs = [joined(a, b) for a, b in zip(pairs[0::2], pairs[1::2])]
    best_ref[0:1, :] = pairs[0][0][:, :tokens]
    best_ref[1:2, :] = pairs[0][1][:, :tokens]

    @pl.loop(1, n_pair)
    def _(k):
        best_copy(k, pair).wait_send()


def fits(n_req, n_seq, shapes):
    residual, query, cache, unembed = shapes
    return (
        n_req % 2 == 0
        and n_seq % 2 == 0
        and query[1] % n_seq == 0
        and query[0] % 16 == 0
        and residual[1] == 64
        and residual[0] == 64
        and cache[1] % 128 == 0
        and unembed[0] % (128 * VOCAB_PIECES) == 0
        and n_req * n_seq & (n_req * n_seq - 1) == 0
    )


def fused(
    n_req,
    n_seq,
    residual,
    query_plain,
    query_rotary,
    latent_cache,
    rotary_cache,
    lengths,
    absorb_key,
    absorb_value,
    output_weight,
    middle_gain,
    routes,
    route_weights,
    gate_weight,
    up_weight,
    down_weight,
    shared_gate,
    shared_up,
    shared_down,
    final_gain,
    unembed,
):
    rows, heads, plain_size = query_plain.shape
    latent = latent_cache.shape[2]
    tokens = residual.shape[0]
    width = unembed.shape[1]
    n_dev = n_req * n_seq
    block_len = latent_cache.shape[1]
    experts, ff = gate_weight.shape[0], gate_weight.shape[2]
    shared_ff = shared_gate.shape[1]
    own_heads = heads // n_seq
    value_size = absorb_value.shape[2]
    parts = latent // 128 + 1
    bf, f32 = jnp.bfloat16, jnp.float32
    dma = pltpu.SemaphoreType.DMA
    vmem = pl.BlockSpec(memory_space=pltpu.VMEM)
    anywhere = pl.BlockSpec(memory_space=pl.ANY)
    layer_out, best = pl.pallas_call(
        functools.partial(layer_kernel, n_req, n_seq),
        name="layer",
        out_shape=(
            jax.ShapeDtypeStruct(residual.shape, bf),
            jax.ShapeDtypeStruct((2, tokens), f32),
        ),
        in_specs=[pl.BlockSpec(memory_space=pltpu.SMEM)] + [vmem] * 7 + [anywhere] * 12,
        out_specs=(vmem, vmem),
        scratch_shapes=[
            pltpu.VMEM((rows, block_len, latent), bf),
            pltpu.VMEM(rotary_cache.shape, bf),
            pltpu.VMEM(absorb_key.shape, bf),
            pltpu.VMEM((rows * heads, plain_size), f32),
            pltpu.VMEM((latent // 128, rows * heads, 128), f32),
            pltpu.VMEM((own_heads, latent, value_size), bf),
            pltpu.VMEM((128, width), bf),
            pltpu.VMEM((2, tokens, 64), bf),
            pltpu.VMEM((experts, ff, width), bf),
            pltpu.VMEM((experts, ff, width), bf),
            pltpu.VMEM((experts, ff, width), bf),
            pltpu.VMEM((shared_ff, width), bf),
            pltpu.VMEM((shared_ff, width), bf),
            pltpu.VMEM((shared_ff, width), bf),
            pltpu.VMEM(unembed.shape, bf),
            pltpu.VMEM((parts, heads * rows, 128), f32),
            pltpu.VMEM((n_seq, parts, own_heads * rows, 128), bf),
            pltpu.VMEM((n_seq, parts, own_heads * rows, 128), bf),
            pltpu.VMEM((rows, own_heads * value_size), bf),
            pltpu.VMEM((tokens // 2, heads * value_size), bf),
            pltpu.VMEM((tokens, width), bf),
            pltpu.VMEM((tokens, width), bf),
            pltpu.VMEM((experts, tokens, 128), f32),
            pltpu.VMEM((tokens, width), f32),
            pltpu.VMEM((tokens // 2, width), bf),
            pltpu.VMEM((tokens // 2, width), bf),
            pltpu.VMEM((tokens // 2, width), bf),
            pltpu.VMEM((n_dev // 2, tokens // 2, 128), bf),
            pltpu.VMEM((tokens, width), bf),
            pltpu.VMEM((8, 128), f32),
            pltpu.VMEM((8, 128), f32),
            pltpu.VMEM((8, 128), f32),
            pltpu.VMEM((n_dev // 2, 8, 128), f32),
            dma((rows,)),
            dma((7,)),
            dma((3, experts)),
            dma((VOCAB_PIECES,)),
            dma((4,)),
            dma((2, n_seq)),
            dma((2, n_dev // 2)),
            dma((2, n_dev // 2 + 1)),
            dma((2, n_dev // 2 + 1)),
            dma((2, n_dev // 2 + 1)),
            dma((2, n_dev // 2 + 1)),
        ],
        compiler_params=pltpu.CompilerParams(
            collective_id=0, has_side_effects=True, vmem_limit_bytes=63 * 1024 * 1024
        ),
    )(
        lengths,
        query_plain,
        query_rotary,
        residual,
        routes.T,
        route_weights.T,
        middle_gain.reshape(1, width),
        final_gain.reshape(1, width),
        latent_cache,
        rotary_cache,
        absorb_key,
        absorb_value,
        output_weight.T,
        jnp.swapaxes(gate_weight, 1, 2),
        jnp.swapaxes(up_weight, 1, 2),
        down_weight,
        shared_gate.T,
        shared_up.T,
        shared_down,
        unembed,
    )
    return layer_out, best.T


def chosen(n_req, n_seq, *args):
    shapes = (args[0].shape, args[1].shape, args[3].shape, args[19].shape)
    if fits(n_req, n_seq, shapes):
        return fused(n_req, n_seq, *args)
    return local(*args)


def solution(mesh):
    in_specs = (
        P(None, ("req", "seq")),
        P("req", None, None),
        P("req", None, None),
        P("req", "seq", None),
        P("req", None, "seq"),
        P("req"),
        P(),
        P(),
        P(None, ("req", "seq")),
        P(),
        P(),
        P(),
        P("seq", None, "req"),
        P("seq", None, "req"),
        P("seq", "req", None),
        P(None, ("req", "seq")),
        P(None, ("req", "seq")),
        P(("req", "seq"), None),
        P(),
        P(("req", "seq"), None),
    )
    out_specs = (P(None, ("req", "seq")), P())
    body = functools.partial(chosen, mesh.shape["req"], mesh.shape["seq"])
    return jax.shard_map(body, mesh=mesh, in_specs=in_specs, out_specs=out_specs, check_vma=False)
```
